256 devices in a mesh: dp: 16 (over z_hi, x), rows: 16 (over y, z_lo, core).
Axes of the slice: x: 4, y: 4, z: 8 (z_hi: 4, z_lo: 2; z = z_hi * 2 + z_lo), core: 2. Of those that a mesh axis runs over, the one named last changes fastest.
Arguments:
- features: bfloat16 [16, 128, 32, 1536], P('dp', 'rows'), may hold values from -6 to 6
- kernel: bfloat16 [7, 7, 1536], replicated, may hold values from -0.875 to 0.875
- ln_gain: float32 [1536], replicated, may hold values from 0.1 to 1.9
- layer_scale: float32 [1536], replicated, may hold values from 0.2 to 1
- w_in: bfloat16 [1536, 3072], P(('dp', 'rows')), may hold values from -0.15625 to 0.15625
- w_out: bfloat16 [3072, 1536], P(('dp', 'rows')), may hold values from -0.109375 to 0.109375
- pairs: int32 [16], replicated, may hold values from 0 to 15, as said below
- negatives: int32 [16, 32, 8, 8], P('dp', 'rows'), may hold values from 0 to 127
Outputs:
- grad_features: bfloat16 [16, 128, 32, 1536], P('dp', 'rows')
- grad_kernel: float32 [7, 7, 1536], replicated
- loss: float32 [], replicated
The draws below stay inside these ranges and needn't reach their ends.
Inputs may be any that keep to these rules, and one draw needn't show every extreme that they name: pairs[pairs[i]] == i and pairs[i] != i: the images form 16 / 2 preference pairs.
All inputs are finite; a program needn't handle non-finite values.
Results may differ from the reference program's by a relative error of at most 0.014.
Values may be sent and summed in bfloat16 or wider, within the bound.
No kernel may reach another device: no remote copies, remote signals or barrier semaphores. Data moves between devices by JAX's collectives and lax.ppermute only.
A program may use at most 128 MiB of HBM per device.

```python
import math
import jax
import jax.numpy as jnp
from jax import lax

C = 1536
FF = 3072
COLS = 32
REGION = 4
NEG = 8
HEIGHT = 128
IMAGES = 16
REG_ROWS = 32
REG_COLS = 8


def draw_pairs(key, part):
    order = jax.random.permutation(key, IMAGES).astype(jnp.int32)
    partner = order.reshape(-1, 2)[:, ::-1].reshape(-1)
    return jnp.zeros((IMAGES,), jnp.int32).at[order].set(partner)


def set_ends(entries, rng, smallest, top_value):
    shape = entries.shape
    index_at = [jax.random.randint(jax.random.fold_in(rng, axis), (), 0, shape[axis]) for axis in range(len(shape))]
    entries = entries.at[tuple(index_at)].set(smallest)
    longest = shape.index(max(shape))
    index_at[longest] = (index_at[longest] + 1) % shape[longest]
    return entries.at[tuple(index_at)].set(top_value)


def levels(key, dims, cuts, smallest, top_value):
    loudness, own = 1.0, jax.random.fold_in(key, 6)
    for axis_at, shards_of in cuts:
        steps = jnp.exp(jax.random.uniform(jax.random.fold_in(own, axis_at), (shards_of,), jnp.float32, smallest / len(cuts), top_value / len(cuts)))
        loudness = loudness * jnp.repeat(steps, dims[axis_at] // shards_of).reshape([-1 if axis == axis_at else 1 for axis in range(len(dims))])
    return loudness


def normal_values(own_key, shape, deviation, most, pieces=(), kind=jnp.bfloat16):
    level = levels(own_key, shape, pieces, -0.22, 0.18) if pieces else 1.0
    values = jax.random.normal(own_key, shape, jnp.float32) * deviation * level
    return jnp.minimum(jnp.maximum(values, -most), most).astype(kind)


def setup_inputs(seed: int = 0) -> dict:
    key_list = jax.random.split(jax.random.key(seed), 9)
    features = normal_values(key_list[0], (IMAGES, HEIGHT, COLS, C), 1.0, 6.0, ((0, 16), (1, 16)))
    kernel = normal_values(key_list[1], (7, 7, C), 49 ** -0.5, 0.875)
    ln_gain = jnp.clip(1.0 + 0.18 * jax.random.normal(key_list[2], (C,), jnp.float32), 0.1, 1.9)
    layer_scale = jnp.clip(jnp.exp(jax.random.uniform(key_list[3], (C,), jnp.float32, math.log(0.2), math.log(1.0))), 0.2, 1.0)
    w_in = normal_values(key_list[4], (C, FF), C ** -0.5, 0.15625, ((0, 256),))
    w_out = normal_values(key_list[5], (FF, C), FF ** -0.5, 0.109375, ((0, 256),))
    pairs = draw_pairs(jax.random.fold_in(key_list[8], 71), 0)
    negatives = set_ends(jax.random.randint(key_list[7], (IMAGES, REG_ROWS, REG_COLS, NEG), 0, IMAGES * REG_COLS), jax.random.fold_in(key_list[7], 1), 0, (IMAGES * REG_COLS) - 1).astype(jnp.int32)
    return dict(features=features, kernel=kernel, ln_gain=ln_gain, layer_scale=layer_scale, w_in=w_in, w_out=w_out, pairs=pairs, negatives=negatives)


loss_scale = 1024.0
inv_temp = 16.0
eps_layer = 1e-06
eps_norm = 1e-06

def depthwise(padded, kernel, height, breadth):
    summed = jnp.zeros((padded.shape[0], height, breadth, padded.shape[3]), jnp.float32)
    for offset_row in range(7):
        for offset_col in range(7):
            window = padded[:, offset_row:offset_row + height, offset_col:offset_col + breadth, :]
            summed = summed + window.astype(jnp.float32) * kernel[offset_row, offset_col].astype(jnp.float32)
    return summed

def kernel_terms(padded, grad_conv, height, breadth):
    grad_float = grad_conv.astype(jnp.float32)
    stacked = []
    for offset_row in range(7):
        row_terms = []
        for offset_col in range(7):
            window = padded[:, offset_row:offset_row + height, offset_col:offset_col + breadth, :]
            row_terms.append(lax.optimization_barrier(jnp.sum(window.astype(jnp.float32) * grad_float, axis=(0, 1, 2))))
        stacked.append(jnp.stack(row_terms))
    return jnp.stack(stacked)

def gelu_parts(pre_act):
    normal_cdf = 0.5 * (1.0 + jax.scipy.special.erf(pre_act * 0.7071067811865476))
    density = jnp.exp(-0.5 * pre_act * pre_act) * 0.3989422804014327
    return (pre_act * normal_cdf, normal_cdf + pre_act * density)

def norm_rows(conv_rows):
    centred = conv_rows - lax.optimization_barrier(jnp.mean(conv_rows, axis=-1, keepdims=True))
    spread = jnp.sqrt(lax.optimization_barrier(jnp.mean(centred * centred, axis=-1, keepdims=True)) + eps_layer)
    return (centred / spread, spread)

def block_forward(one_image, kernel, ln_gain, layer_scale, w_in, w_out):
    height, breadth, channels = one_image.shape
    padded = jnp.pad(one_image, ((3, 3), (3, 3), (0, 0)))[None]
    conv_rows = depthwise(padded, kernel, height, breadth).reshape(-1, channels)
    unit_rows, spread = norm_rows(conv_rows)
    normed = (unit_rows * ln_gain).astype(jnp.bfloat16)
    pre_act = jnp.dot(normed, w_in, preferred_element_type=jnp.float32)
    activated, gelu_slope = gelu_parts(pre_act)
    hidden = activated.astype(jnp.bfloat16)
    mixed_rows = jnp.dot(hidden, w_out, preferred_element_type=jnp.float32)
    block_out = one_image.reshape(-1, channels).astype(jnp.float32) + layer_scale * mixed_rows
    return (padded, unit_rows, spread, gelu_slope, block_out)

def pool_tokens(block_out, height, breadth, channels):
    blocks = block_out.reshape(height // REGION, REGION, breadth // REGION, REGION, channels)
    return lax.optimization_barrier(jnp.mean(blocks, axis=(1, 3)))

def expand_grad(grad_pool, height, breadth, channels):
    scaled = grad_pool / float(REGION * REGION)
    spread_out = jnp.broadcast_to(scaled[:, None, :, None, :], (height // REGION, REGION, breadth // REGION, REGION, channels))
    return spread_out.reshape(height * breadth, channels)

def conv_grad(grad_unit, unit_rows, spread):
    mean_one = lax.optimization_barrier(jnp.mean(grad_unit, axis=-1, keepdims=True))
    mean_two = lax.optimization_barrier(jnp.mean(grad_unit * unit_rows, axis=-1, keepdims=True))
    return (grad_unit - mean_one - unit_rows * mean_two) / spread

def reference(features, kernel, ln_gain, layer_scale, w_in, w_out, pairs, negatives):
    images, height, breadth, channels = features.shape

    def tokens_of(one_image):
        parts = block_forward(one_image, kernel, ln_gain, layer_scale, w_in, w_out)
        return pool_tokens(parts[4], height, breadth, channels)
    pooled = lax.map(tokens_of, features)
    reg_rows, reg_cols = (pooled.shape[1], pooled.shape[2])
    inv_norm = lax.rsqrt(lax.optimization_barrier(jnp.sum(pooled * pooled, axis=-1, keepdims=True)) + eps_norm)
    unit_tok = pooled * inv_norm
    tokens_b = unit_tok.astype(jnp.bfloat16)
    keys_flat = tokens_b.transpose(1, 0, 2, 3).reshape(reg_rows, images * reg_cols, channels)
    columns = jnp.arange(reg_cols, dtype=jnp.int32)
    positive = pairs.astype(jnp.int32)[:, None] * reg_cols + columns[None, :]
    positive = jnp.broadcast_to(positive[:, None, :, None], (images, reg_rows, reg_cols, 1))
    chosen = jnp.concatenate([positive, negatives.astype(jnp.int32)], axis=3)
    row_index = jnp.arange(reg_rows, dtype=jnp.int32)[None, :, None, None]
    picked = keys_flat[row_index, chosen].astype(jnp.float32)
    tokens_f = tokens_b.astype(jnp.float32)
    logits = inv_temp * jnp.einsum('irtc,irtkc->irtk', tokens_f, picked, precision=lax.Precision.HIGHEST)
    exp_logits = jnp.exp(logits)
    denominator = lax.optimization_barrier(jnp.sum(exp_logits, axis=-1, keepdims=True))
    loss_tok = jnp.log(denominator[..., 0]) - logits[..., 0]
    loss = jnp.mean(loss_tok)
    first_slot = (jnp.arange(NEG + 1) == 0).astype(jnp.float32)
    slot_coef = loss_scale * inv_temp * (exp_logits / denominator - first_slot)
    anchor = jnp.einsum('irtk,irtkc->irtc', slot_coef, picked, precision=lax.Precision.HIGHEST)
    contrib = slot_coef[..., None] * tokens_f[:, :, :, None, :]
    key_table = jnp.zeros((reg_rows, images * reg_cols, channels), jnp.float32).at[row_index, chosen].add(contrib)
    key_table = key_table.reshape(reg_rows, images, reg_cols, channels).transpose(1, 0, 2, 3)
    grad_tok = anchor + key_table
    grad_pool = (grad_tok - unit_tok * lax.optimization_barrier(jnp.sum(unit_tok * grad_tok, axis=-1, keepdims=True))) * inv_norm

    def backward_of(packed):
        one_image, one_grad = packed
        padded, unit_rows, spread, gelu_slope, block_out = block_forward(one_image, kernel, ln_gain, layer_scale, w_in, w_out)
        grad_out = expand_grad(one_grad, height, breadth, channels)
        grad_mix = (layer_scale * grad_out).astype(jnp.bfloat16)
        grad_hid = lax.dot_general(grad_mix, w_out, (((1,), (1,)), ((), ())), preferred_element_type=jnp.float32)
        grad_pre = (grad_hid * gelu_slope).astype(jnp.bfloat16)
        grad_norm = lax.dot_general(grad_pre, w_in, (((1,), (1,)), ((), ())), preferred_element_type=jnp.float32)
        grad_conv = conv_grad(grad_norm * ln_gain, unit_rows, spread).astype(jnp.bfloat16).reshape(1, height, breadth, channels)
        grad_pad = jnp.pad(grad_conv, ((0, 0), (3, 3), (3, 3), (0, 0)))
        conv_back = depthwise(grad_pad, kernel[::-1, ::-1], height, breadth)
        grad_feat = (grad_out.reshape(1, height, breadth, channels) + conv_back).astype(jnp.bfloat16)[0]
        return (grad_feat, kernel_terms(padded, grad_conv, height, breadth))
    grad_features, kernel_parts = lax.map(backward_of, (features, grad_pool))
    grad_kernel = lax.optimization_barrier(jnp.sum(kernel_parts, axis=0))
    return (grad_features, grad_kernel, loss)
```

```python
import jax
import jax.numpy as jnp
from jax import lax
from jax.experimental import pallas as pl
from jax.experimental.pallas import tpu as pltpu
from jax.sharding import Mesh, PartitionSpec as P

REGION = 4
NEG = 8
loss_scale = 1024.0
inv_temp = 16.0
eps_layer = 1e-06
eps_norm = 1e-06

AXES = ("z_hi", "x", "y", "z_lo", "core")
DP = ("z_hi", "x")
ROWS = ("y", "z_lo", "core")
bf16 = jnp.bfloat16
f32 = jnp.float32
ANY = pl.BlockSpec(memory_space=pl.ANY)
SMEM = pl.BlockSpec(memory_space=pltpu.SMEM)


def fetch(value, axis, count, distance):
    return lax.ppermute(value, axis, [((i + distance) % count, i) for i in range(count)])


def direct4(value, axis):
    return jnp.stack([value] + [fetch(value, axis, 4, d) for d in (1, 2, 3)])


def ring4(value, axis):
    half = value.shape[0] // 2
    ahead = fetch(value, axis, 4, 1)
    behind = fetch(value, axis, 4, 3)
    far_low = fetch(ahead[:half], axis, 4, 1)
    far_high = fetch(behind[half:], axis, 4, 3)
    return [value, ahead, far_low, far_high, behind]


def joined(pieces):
    own, ahead, far_low, far_high, behind = pieces
    return jnp.stack([own, ahead, jnp.concatenate([far_low, far_high]), behind])


def both_cores(pieces):
    return list(pieces) + [fetch(piece, "core", 2, 1) for piece in pieces]


def core_half(shard):
    chip = lax.all_gather(shard, "core", axis=0, tiled=True)
    width = chip.shape[1] // 2
    half = jnp.where(lax.axis_index("core") == 0, chip[:, :width], chip[:, width:])
    other = fetch(half, "z_lo", 2, 1)
    return jnp.where(
        lax.axis_index("z_lo") == 0,
        jnp.concatenate([half, other]),
        jnp.concatenate([other, half]),
    )


def rotated(stack, axis):
    twice = jnp.concatenate([stack, stack])
    return lax.dynamic_slice_in_dim(twice, 4 - lax.axis_index(axis), 4)


def gather_in(shard):
    block = core_half(shard)
    near = rotated(direct4(block, "y"), "y")
    near = near.reshape(-1, near.shape[-1])
    middle = joined(ring4(near[None].reshape(2, -1, near.shape[-1]), "z_hi"))
    middle = middle.reshape(4, -1, near.shape[-1])
    return both_cores(ring4(middle, "x"))


def gather_out(shard):
    block = core_half(shard)
    near = direct4(block, "z_hi")
    middle = joined(ring4(near, "x"))
    return both_cores(ring4(middle, "y"))


FAR = ((0, 0), (1, 0), (2, 0), (2, 2), (3, 0))


def copies_in(idx, pieces, held, sems):
    z, x = idx[0], idx[1]
    for core in range(2):
        for (far, base), piece in zip(FAR, pieces[core * 5 : core * 5 + 5]):
            for i in range(piece.shape[0]):
                rows = piece.shape[1]
                at = (((z + base + i) % 4) * 4 + (x + far) % 4) * rows
                pltpu.make_async_copy(
                    piece.at[i],
                    held.at[core, pl.ds(pl.multiple_of(at, rows), rows), :],
                    sems.at[core],
                ).start()


def copies_out(idx, pieces, held, sems):
    z, x, y = idx[0], idx[1], idx[2]
    for core in range(2):
        for (far, base), piece in zip(FAR, pieces[core * 5 : core * 5 + 5]):
            for i in range(piece.shape[0]):
                for j in range(4):
                    rows = piece.shape[2]
                    at = (
                        (((z + j) % 4) * 4 + (x + base + i) % 4) * 4 + (y + far) % 4
                    ) * rows
                    pltpu.make_async_copy(
                        piece.at[i, j],
                        held.at[core, pl.ds(pl.multiple_of(at, rows), rows), :],
                        sems.at[core],
                    ).start()


def arrive(held, sems, core):
    pltpu.make_async_copy(held.at[core], held.at[core], sems.at[core]).wait()


def region_of(pixel):
    return ((pixel >> 7) << 3) + ((pixel & 31) >> 2)


def split2(value):
    high = value.astype(bf16)
    return high, (value - high.astype(f32)).astype(bf16)


def split3(value):
    high = value.astype(bf16)
    rest = value - high.astype(f32)
    mid = rest.astype(bf16)
    return high, mid, (rest - mid.astype(f32)).astype(bf16)


def pool_matrix(tokens, pixels):
    token = lax.broadcasted_iota(jnp.int32, (tokens, pixels), 0)
    pixel = lax.broadcasted_iota(jnp.int32, (tokens, pixels), 1)
    return jnp.where(region_of(pixel) == token, 1.0 / 16.0, 0.0).astype(bf16)


def dot(a, b):
    return jnp.dot(a, b, preferred_element_type=f32)


def dot_t(a, b):
    return lax.dot_general(a, b, (((1,), (1,)), ((), ())), preferred_element_type=f32)


def first_kernel(idx, normed, *refs):
    pieces, (slope, pooled, held, sems) = refs[:10], refs[10:]
    copies_in(idx, pieces, held, sems)
    pixels = normed.shape[0]
    pool = pool_matrix(pooled.shape[1] // 2, pixels)
    tokens = pool.shape[0]
    for core in range(2):
        arrive(held, sems, core)
        at = (idx[4] + core) % 2
        for n in range(0, held.shape[2], 512):
            pre = dot(normed[...], held[core, :, n : n + 512])
            cdf = 0.5 * (1.0 + lax.erf(pre * 0.7071067811865476))
            density = jnp.exp(-0.5 * pre * pre) * 0.3989422804014327
            hidden = (pre * cdf).astype(bf16)
            slope[at, :, n : n + 512] = cdf + pre * density
            high, low = split2(dot(pool, hidden))
            pooled[at, :tokens, n : n + 512] = high
            pooled[at, tokens:, n : n + 512] = low


def second_kernel(idx, hidden, feats, scale, *refs):
    pieces, (unit, norm, token, held, mixed, sems) = refs[:10], refs[10:]
    copies_out(idx, pieces, held, sems)
    tokens = unit.shape[0]
    base = dot(pool_matrix(tokens, feats.shape[0]), feats[...])
    half = hidden.shape[2]
    for core in range(2):
        arrive(held, sems, core)
        at = (idx[4] + core) % 2
        both = dot(hidden[0], held[core, :half, :]) + dot(hidden[1], held[core, half:, :])
        mixed[at] = both[:tokens] + both[tokens:]
    full = jnp.concatenate([mixed[0], mixed[1]], axis=1)
    pool = base + scale[...] * full
    inv = lax.rsqrt(jnp.sum(pool * pool, axis=1, keepdims=True) + eps_norm)
    unit[...] = pool * inv
    norm[...] = jnp.broadcast_to(inv, norm.shape)
    token[...] = (pool * inv).astype(bf16)


def third_kernel(
    idx, keys, chosen, ids, unit, norm, scale, gain, spread, slope_hbm, rows_hbm, *refs
):
    out_pieces, in_pieces = refs[:10], refs[10:20]
    (grad_conv, scaled, loss, held_out, held_in, slope, rows, mix, hid, sem_out, sem_in, sem) = (
        refs[20:]
    )
    copies_out(idx, out_pieces, held_out, sem_out)
    copies_in(idx, in_pieces, held_in, sem_in)
    copy_slope = pltpu.make_async_copy(slope_hbm, slope, sem.at[0])
    copy_slope.start()
    copy_rows = pltpu.make_async_copy(rows_hbm, rows, sem.at[1])
    copy_rows.start()
    token_grads, losses = [], []
    for r in range(keys.shape[0]):
        key = keys[r]
        count = key.shape[0]
        similar = dot_t(key, key)
        hits, logits = [], []
        for n in range(NEG + 1):
            hit = chosen[r, :, n : n + 1] == ids[...]
            hits.append(hit)
            logits.append(
                inv_temp * jnp.sum(jnp.where(hit, similar, 0.0), axis=1, keepdims=True)
            )
        exps = [jnp.exp(value) for value in logits]
        total = exps[0]
        for value in exps[1:]:
            total = total + value
        weight = jnp.zeros((count, count), f32)
        for n in range(NEG + 1):
            coef = loss_scale * inv_temp * (exps[n] / total - (1.0 if n == 0 else 0.0))
            weight = weight + jnp.where(hits[n], coef, 0.0)
        own = weight[:8] + jnp.transpose(weight)[:8]
        high, mid, low = split3(own)
        token_grads.append(dot(high, key) + dot(mid, key) + dot(low, key))
        losses.append((jnp.log(total) - logits[0])[:8])
    loss[...] = jnp.broadcast_to(
        jnp.sum(losses[0] + losses[1], axis=0, keepdims=True), loss.shape
    )
    grad_tok = jnp.concatenate(token_grads, axis=0)
    unit_v = unit[...]
    grad_pool = (grad_tok - unit_v * jnp.sum(unit_v * grad_tok, axis=1, keepdims=True)) * norm[
        :, :1
    ]
    spread_grad = grad_pool / 16.0
    scaled[...] = spread_grad
    grad_mix = (scale[...] * spread_grad).astype(bf16)
    width = held_out.shape[2]
    mix[0] = grad_mix[:, :width]
    mix[1] = grad_mix[:, width:]
    part = None
    for core in range(2):
        arrive(held_out, sem_out, core)
        at = (idx[4] + core) % 2
        term = dot_t(mix[at], held_out[core])
        part = term if part is None else part + term
    half = held_in.shape[2]
    hid[0] = part[:, :half]
    hid[1] = part[:, half:]
    copy_slope.wait()
    pixels, tokens = rows.shape[0], part.shape[0]
    pixel = lax.broadcasted_iota(jnp.int32, (pixels, 3 * tokens), 0)
    token = lax.broadcasted_iota(jnp.int32, (pixels, 3 * tokens), 1) % tokens
    expand = jnp.where(region_of(pixel) == token, 1.0, 0.0).astype(bf16)
    total = None
    for core in range(2):
        arrive(held_in, sem_in, core)
        at = (idx[4] + core) % 2
        wide = dot(expand, jnp.concatenate(split3(hid[at]), axis=0))
        grad_pre = (wide * slope[at]).astype(bf16)
        term = dot_t(grad_pre, held_in[core])
        total = term if total is None else total + term
    copy_rows.wait()
    grad_unit = total * gain[...]
    unit_rows = rows[...]
    mean_one = jnp.mean(grad_unit, axis=1, keepdims=True)
    mean_two = jnp.mean(grad_unit * unit_rows, axis=1, keepdims=True)
    grad_conv[...] = ((grad_unit - mean_one - unit_rows * mean_two) / spread[:, :1]).astype(bf16)


def padded_rows(cells, width):
    count = lax.axis_size(ROWS)
    ends = count - 1
    head = cells[:, :width]
    tail = cells[:, cells.shape[1] - width :]
    return jnp.concatenate(
        [
            lax.ppermute(tail, ROWS, [(i, i + 1) for i in range(ends)]),
            cells,
            lax.ppermute(head, ROWS, [(i + 1, i) for i in range(ends)]),
        ],
        axis=1,
    )


def depthwise(padded, kernel, height, breadth):
    summed = jnp.zeros((padded.shape[0], height, breadth, padded.shape[3]), f32)
    for offset_row in range(7):
        for offset_col in range(7):
            window = padded[
                :, offset_row : offset_row + height, offset_col : offset_col + breadth, :
            ]
            summed = summed + window.astype(f32) * kernel[offset_row, offset_col].astype(f32)
    return summed


def kernel_terms(padded, grad_conv, height, breadth):
    grad_float = grad_conv.astype(f32)
    stacked = []
    for offset_row in range(7):
        for offset_col in range(7):
            window = padded[
                :, offset_row : offset_row + height, offset_col : offset_col + breadth, :
            ]
            stacked.append(jnp.sum(window.astype(f32) * grad_float, axis=(0, 1, 2)))
    return jnp.stack(stacked)


def gather_tokens(message):
    near = [message] + [fetch(message, "z_hi", 4, d) for d in (1, 2, 3)]
    near = jnp.concatenate(near, axis=1)
    ahead = fetch(near, "x", 4, 1)
    behind = fetch(near, "x", 4, 3)
    far = fetch(near, "x", 4, 2)
    return jnp.concatenate([near, ahead, far, behind], axis=1)


def all_sum(values):
    count = lax.axis_size(AXES)
    split = values.reshape(count, -1)
    mine = jnp.sum(lax.all_to_all(split, AXES, 0, 0), axis=0, keepdims=True)
    return lax.all_to_all(jnp.broadcast_to(mine, split.shape), AXES, 0, 0).reshape(values.shape)


def params(name, megabytes):
    return dict(
        name=name, compiler_params=pltpu.CompilerParams(vmem_limit_bytes=megabytes << 20)
    )


def body(features, kernel, ln_gain, layer_scale, w_in, w_out, pairs, negatives):
    height, breadth, channels = (features.shape[1], features.shape[2], features.shape[3])
    pixels = height * breadth
    reg_rows, reg_cols = (height // REGION, breadth // REGION)
    tokens = reg_rows * reg_cols
    hidden_width = w_in.shape[1]
    z, x, y, core = (lax.axis_index(name) for name in ("z_hi", "x", "y", "core"))
    idx = jnp.stack([z, x, y, lax.axis_index("z_lo"), core]).astype(jnp.int32)

    rimmed = padded_rows(features, 3)
    in_pieces = gather_in(w_in)
    out_pieces = gather_out(w_out)

    padded = jnp.pad(rimmed, ((0, 0), (0, 0), (3, 3), (0, 0)))
    conv_rows = depthwise(padded, kernel, height, breadth).reshape(-1, channels)
    centred = conv_rows - jnp.mean(conv_rows, axis=-1, keepdims=True)
    spread = jnp.sqrt(jnp.mean(centred * centred, axis=-1, keepdims=True) + eps_layer)
    unit_rows = centred / spread
    normed = (unit_rows * ln_gain).astype(bf16)

    half = hidden_width // 2
    slope, pooled_hidden = pl.pallas_call(
        first_kernel,
        out_shape=(
            jax.ShapeDtypeStruct((2, pixels, half), f32),
            jax.ShapeDtypeStruct((2, 2 * tokens, half), bf16),
        ),
        in_specs=[SMEM, pl.BlockSpec()] + [ANY] * 10,
        scratch_shapes=[
            pltpu.VMEM((2, channels, half), bf16),
            pltpu.SemaphoreType.DMA((2,)),
        ],
        **params("expand_rows", 48),
    )(idx, normed, *in_pieces)

    width = channels // 2
    unit_tok, inv_norm, tokens_b = pl.pallas_call(
        second_kernel,
        out_shape=(
            jax.ShapeDtypeStruct((tokens, channels), f32),
            jax.ShapeDtypeStruct((tokens, 128), f32),
            jax.ShapeDtypeStruct((tokens, channels), bf16),
        ),
        in_specs=[SMEM] + [pl.BlockSpec()] * 3 + [ANY] * 10,
        scratch_shapes=[
            pltpu.VMEM((2, hidden_width, width), bf16),
            pltpu.VMEM((2, tokens, width), f32),
            pltpu.SemaphoreType.DMA((2,)),
        ],
        **params("pool_tokens", 32),
    )(
        idx,
        pooled_hidden,
        features.reshape(pixels, channels),
        layer_scale.reshape(1, channels),
        *out_pieces,
    )

    message = jnp.concatenate(
        [
            tokens_b.reshape(reg_rows, reg_cols, channels),
            jnp.pad(negatives[0].astype(bf16), ((0, 0), (0, 0), (0, 128 - NEG))),
        ],
        axis=2,
    )
    gathered = gather_tokens(message)
    keys = gathered[:, :, :channels]
    slot = jnp.arange(16, dtype=jnp.int32)
    image = ((z + slot % 4) % 4) * 4 + (x + slot // 4) % 4
    columns = jnp.arange(reg_cols, dtype=jnp.int32)
    ids = (image[:, None] * reg_cols + columns[None, :]).reshape(1, -1)
    positive = (pairs[image][:, None] * reg_cols + columns[None, :]).reshape(1, -1, 1)
    chosen = jnp.concatenate(
        [
            jnp.broadcast_to(positive, (reg_rows, positive.shape[1], 1)),
            gathered[:, :, channels : channels + NEG].astype(jnp.int32),
        ],
        axis=2,
    )

    grad_conv, scaled, loss_part = pl.pallas_call(
        third_kernel,
        out_shape=(
            jax.ShapeDtypeStruct((pixels, channels), bf16),
            jax.ShapeDtypeStruct((tokens, channels), f32),
            jax.ShapeDtypeStruct((1, 128), f32),
        ),
        in_specs=[SMEM] + [pl.BlockSpec()] * 8 + [ANY] * 22,
        scratch_shapes=[
            pltpu.VMEM((2, hidden_width, width), bf16),
            pltpu.VMEM((2, channels, half), bf16),
            pltpu.VMEM((2, pixels, half), f32),
            pltpu.VMEM((pixels, channels), f32),
            pltpu.VMEM((2, tokens, width), bf16),
            pltpu.VMEM((2, tokens, half), f32),
            pltpu.SemaphoreType.DMA((2,)),
            pltpu.SemaphoreType.DMA((2,)),
            pltpu.SemaphoreType.DMA((2,)),
        ],
        **params("loss_and_back", 58),
    )(
        idx,
        keys,
        chosen,
        ids,
        unit_tok,
        inv_norm,
        layer_scale.reshape(1, channels),
        ln_gain.reshape(1, channels),
        jnp.broadcast_to(spread, (pixels, 128)),
        slope,
        unit_rows,
        *out_pieces,
        *in_pieces,
    )

    grad_conv = grad_conv.reshape(1, height, breadth, channels)
    kernel_local = kernel_terms(padded, grad_conv, height, breadth)
    loss_row = jnp.pad(loss_part[:, :1], ((0, 14), (0, channels - 1)))
    summed = all_sum(jnp.concatenate([kernel_local, loss_row], axis=0))

    grad_rim = padded_rows(grad_conv, 3)
    grad_pad = jnp.pad(grad_rim, ((0, 0), (0, 0), (3, 3), (0, 0)))
    conv_back = depthwise(grad_pad, kernel[::-1, ::-1], height, breadth)
    grad_out = jnp.broadcast_to(
        scaled.reshape(reg_rows, 1, reg_cols, 1, channels),
        (reg_rows, REGION, reg_cols, REGION, channels),
    ).reshape(1, height, breadth, channels)
    grad_features = (grad_out + conv_back).astype(bf16)

    grad_kernel = summed[:49].reshape(7, 7, channels)
    token_count = lax.axis_size(AXES) * tokens
    loss = summed[49, 0] / float(token_count)
    return (grad_features, grad_kernel, loss)


def solution(mesh):
    split = Mesh(mesh.devices.reshape(4, 4, 4, 2, 2), AXES)
    return jax.shard_map(
        body,
        mesh=split,
        in_specs=(
            P(DP, ROWS, None, None),
            P(),
            P(),
            P(),
            P(AXES, None),
            P(AXES, None),
            P(),
            P(DP, ROWS, None, None),
        ),
        out_specs=(P(DP, ROWS, None, None), P(), P()),
        check_vma=False,
    )
```

```python
import jax
import jax.numpy as jnp
from jax import lax
from jax.experimental import pallas as pl
from jax.experimental.pallas import tpu as pltpu
from jax.sharding import Mesh, PartitionSpec as P

REGION = 4
NEG = 8
loss_scale = 1024.0
inv_temp = 16.0
eps_layer = 1e-06
eps_norm = 1e-06

AXES = ("z_hi", "x", "y", "z_lo", "core")
DP = ("z_hi", "x")
ROWS = ("y", "z_lo", "core")
bf16 = jnp.bfloat16
f32 = jnp.float32
ANY = pl.BlockSpec(memory_space=pl.ANY)
SMEM = pl.BlockSpec(memory_space=pltpu.SMEM)


def fetch(value, axis, count, distance):
    return lax.ppermute(value, axis, [((i + distance) % count, i) for i in range(count)])


def ring_first(value, axis):
    return fetch(value, axis, 4, 1), fetch(value, axis, 4, 3)


def ring_second(value, ahead, behind, axis):
    half = value.shape[0] // 2
    far_low = fetch(ahead[:half], axis, 4, 1)
    far_high = fetch(behind[half:], axis, 4, 3)
    return [value, ahead, far_low, far_high, behind]


def both_cores(pieces):
    return list(pieces) + [fetch(piece, "core", 2, 1) for piece in pieces]


def along_z(w_in, w_out):
    rows, width = w_in.shape[0], w_in.shape[1] // 2
    narrow = w_out.shape[1] // 2
    halves = [
        jnp.concatenate(
            [
                w_in[:, c * width : (c + 1) * width],
                w_out[:rows, c * narrow : (c + 1) * narrow],
                w_out[rows:, c * narrow : (c + 1) * narrow],
            ],
            axis=1,
        )
        for c in range(2)
    ]
    message = jnp.stack(halves)
    message = jnp.broadcast_to(message[None], (8,) + message.shape).reshape(16, rows, -1)
    got = lax.all_to_all(message, ("z_hi", "z_lo", "core"), 0, 0)
    near_in = got[:, :, :width].reshape(4, 4 * rows, width)
    near_out = jnp.concatenate(
        [got[:, :, width : width + narrow], got[:, :, width + narrow :]], axis=1
    ).reshape(4, 8 * rows, narrow)
    return near_in, near_out


def gather_weights(w_in, w_out, other_work):
    y = lax.axis_index("y")
    near_in, near_out = along_z(w_in, w_out)
    first_in = ring_first(near_in, "y")
    first_out = ring_first(near_out, "x")
    own, ahead, low, high, behind = ring_second(near_in, *first_in, "y")
    middle_in = jnp.zeros((4, 4) + near_in.shape[1:], near_in.dtype)
    for piece, far in (
        (own, 0),
        (ahead, 1),
        (behind, 3),
        (jnp.concatenate([low, high]), 2),
    ):
        middle_in = lax.dynamic_update_slice(middle_in, piece[:, None], (0, (y + far) % 4, 0, 0))
    middle_in = middle_in.reshape(4, -1, near_in.shape[2])
    own, ahead, low, high, behind = ring_second(near_out, *first_out, "x")
    middle_out = jnp.stack([own, ahead, jnp.concatenate([low, high]), behind])
    first_in = ring_first(middle_in, "x")
    first_out = ring_first(middle_out, "y")
    first_in, first_out, other_work = lax.optimization_barrier((first_in, first_out, other_work))
    pieces_in = both_cores(ring_second(middle_in, *first_in, "x"))
    pieces_out = both_cores(ring_second(middle_out, *first_out, "y"))
    return pieces_in, pieces_out, other_work


FAR = ((0, 0), (1, 0), (2, 0), (2, 2), (3, 0))


def copies_in(idx, pieces, held, sems):
    x = idx[1]
    for core in range(2):
        for (far, base), piece in zip(FAR, pieces[core * 5 : core * 5 + 5]):
            rows = piece.shape[1]
            for i in range(piece.shape[0]):
                at = ((base + i) * 4 + (x + far) % 4) * rows
                pltpu.make_async_copy(
                    piece.at[i],
                    held.at[core, pl.ds(pl.multiple_of(at, rows), rows), :],
                    sems.at[core],
                ).start()


def copies_out(idx, pieces, held, sems):
    x, y = idx[1], idx[2]
    for core in range(2):
        for (far, base), piece in zip(FAR, pieces[core * 5 : core * 5 + 5]):
            for i in range(piece.shape[0]):
                pltpu.make_async_copy(
                    piece.at[i],
                    held.at[core, :, (x + base + i) % 4, (y + far) % 4],
                    sems.at[core],
                ).start()


def arrive(held, sems, core):
    pltpu.make_async_copy(held.at[core], held.at[core], sems.at[core]).wait()


def region_of(pixel):
    return ((pixel >> 7) << 3) + ((pixel & 31) >> 2)


def split2(value):
    high = value.astype(bf16)
    return high, (value - high.astype(f32)).astype(bf16)


def split3(value):
    high = value.astype(bf16)
    rest = value - high.astype(f32)
    mid = rest.astype(bf16)
    return high, mid, (rest - mid.astype(f32)).astype(bf16)


def pool_matrix(tokens, pixels):
    token = lax.broadcasted_iota(jnp.int32, (tokens, pixels), 0)
    pixel = lax.broadcasted_iota(jnp.int32, (tokens, pixels), 1)
    return jnp.where(region_of(pixel) == token, 1.0 / 16.0, 0.0).astype(bf16)


def dot(a, b):
    return jnp.dot(a, b, preferred_element_type=f32)


def dot_t(a, b):
    return lax.dot_general(a, b, (((1,), (1,)), ((), ())), preferred_element_type=f32)


def first_kernel(idx, normed, *refs):
    pieces, (slope, pooled, held, sems) = refs[:10], refs[10:]
    copies_in(idx, pieces, held, sems)
    pixels = normed.shape[0]
    tokens = pooled.shape[1] // 2
    steps = held.shape[2] // 512

    for core in range(2):
        arrive(held, sems, core)
        at = (idx[4] + core) % 2

        @pl.loop(0, steps)
        def _(step):
            lanes = pl.ds(pl.multiple_of(step * 512, 512), 512)
            pre = dot(normed[...], held[core, :, lanes])
            cdf = 0.5 * (1.0 + lax.erf(pre * 0.7071067811865476))
            density = jnp.exp(-0.5 * pre * pre) * 0.3989422804014327
            hidden = (pre * cdf).astype(bf16)
            slope[at, :, lanes] = cdf + pre * density
            high, low = split2(dot(pool_matrix(tokens, pixels), hidden))
            pooled[at, :tokens, lanes] = high
            pooled[at, tokens:, lanes] = low


def second_kernel(idx, hidden, feats, scale, *refs):
    pieces, (unit, norm, token, held, mixed, sems) = refs[:10], refs[10:]
    copies_out(idx, pieces, held, sems)
    tokens = unit.shape[0]
    base = dot(pool_matrix(tokens, feats.shape[0]), feats[...])
    half, width = hidden.shape[2], held.shape[5]
    for core in range(2):
        arrive(held, sems, core)
        at = (idx[4] + core) % 2
        low = held[core, :2].reshape(half, width)
        high = held[core, 2:].reshape(half, width)
        both = dot(hidden[0], low) + dot(hidden[1], high)
        mixed[at] = both[:tokens] + both[tokens:]
    full = jnp.concatenate([mixed[0], mixed[1]], axis=1)
    pool = base + scale[...] * full
    inv = lax.rsqrt(jnp.sum(pool * pool, axis=1, keepdims=True) + eps_norm)
    unit[...] = pool * inv
    norm[...] = jnp.broadcast_to(inv, norm.shape)
    token[...] = (pool * inv).astype(bf16)


def third_kernel(
    idx, keys, chosen, ids, unit, norm, scale, gain, spread, slope_hbm, rows_hbm, *refs
):
    out_pieces, in_pieces = refs[:10], refs[10:20]
    (grad_conv, scaled, loss, held_out, held_in, slope, rows, mix, hid, total_ref) = refs[20:30]
    sem_out, sem_in, sem = refs[30:]
    copies_out(idx, out_pieces, held_out, sem_out)
    copies_in(idx, in_pieces, held_in, sem_in)
    copy_slope = pltpu.make_async_copy(slope_hbm, slope, sem.at[0])
    copy_slope.start()
    copy_rows = pltpu.make_async_copy(rows_hbm, rows, sem.at[1])
    copy_rows.start()
    token_grads, losses = [], []
    for r in range(keys.shape[0]):
        key = keys[r]
        count = key.shape[0]
        similar = dot_t(key, key)
        hits, logits = [], []
        for n in range(NEG + 1):
            hit = chosen[r, :, n : n + 1] == ids[...]
            hits.append(hit)
            logits.append(
                inv_temp * jnp.sum(jnp.where(hit, similar, 0.0), axis=1, keepdims=True)
            )
        exps = [jnp.exp(value) for value in logits]
        total = exps[0]
        for value in exps[1:]:
            total = total + value
        weight = jnp.zeros((count, count), f32)
        for n in range(NEG + 1):
            coef = loss_scale * inv_temp * (exps[n] / total - (1.0 if n == 0 else 0.0))
            weight = weight + jnp.where(hits[n], coef, 0.0)
        own = weight[:8] + jnp.transpose(weight)[:8]
        high, mid, low = split3(own)
        token_grads.append(dot(high, key) + dot(mid, key) + dot(low, key))
        losses.append((jnp.log(total) - logits[0])[:8])
    loss[...] = jnp.broadcast_to(
        jnp.sum(losses[0] + losses[1], axis=0, keepdims=True), loss.shape
    )
    grad_tok = jnp.concatenate(token_grads, axis=0)
    unit_v = unit[...]
    grad_pool = (grad_tok - unit_v * jnp.sum(unit_v * grad_tok, axis=1, keepdims=True)) * norm[
        :, :1
    ]
    spread_grad = grad_pool / 16.0
    scaled[...] = spread_grad
    grad_mix = (scale[...] * spread_grad).astype(bf16)
    width = held_out.shape[5]
    mix[0] = grad_mix[:, :width]
    mix[1] = grad_mix[:, width:]
    part = None
    for core in range(2):
        arrive(held_out, sem_out, core)
        at = (idx[4] + core) % 2
        term = dot_t(held_out[core].reshape(-1, width), mix[at])
        part = term if part is None else part + term
    half = held_in.shape[2]
    tokens = part.shape[1]
    for k in range(2):
        for i, piece in enumerate(split3(jnp.transpose(part[k * half : (k + 1) * half]))):
            hid[k, i * tokens : (i + 1) * tokens] = piece
    copy_slope.wait()
    pixels = rows.shape[0]
    total_ref[...] = jnp.zeros(total_ref.shape, f32)
    for core in range(2):
        arrive(held_in, sem_in, core)
        at = (idx[4] + core) % 2

        @pl.loop(0, half // 512)
        def _(step):
            lanes = pl.ds(pl.multiple_of(step * 512, 512), 512)
            pixel = lax.broadcasted_iota(jnp.int32, (pixels, 3 * tokens), 0)
            token = lax.broadcasted_iota(jnp.int32, (pixels, 3 * tokens), 1) & (tokens - 1)
            expand = jnp.where(region_of(pixel) == token, 1.0, 0.0).astype(bf16)
            wide = dot(expand, hid[at, :, lanes])
            grad_pre = (wide * slope[at, :, lanes]).astype(bf16)
            total_ref[...] += dot_t(grad_pre, held_in[core, :, lanes])

    copy_rows.wait()
    grad_unit = total_ref[...] * gain[...]
    unit_rows = rows[...]
    mean_one = jnp.mean(grad_unit, axis=1, keepdims=True)
    mean_two = jnp.mean(grad_unit * unit_rows, axis=1, keepdims=True)
    grad_conv[...] = ((grad_unit - mean_one - unit_rows * mean_two) / spread[:, :1]).astype(bf16)


def padded_rows(cells, width):
    count = lax.axis_size(ROWS)
    ends = count - 1
    head = cells[:, :width]
    tail = cells[:, cells.shape[1] - width :]
    return jnp.concatenate(
        [
            lax.ppermute(tail, ROWS, [(i, i + 1) for i in range(ends)]),
            cells,
            lax.ppermute(head, ROWS, [(i + 1, i) for i in range(ends)]),
        ],
        axis=1,
    )


def depthwise(padded, kernel, height, breadth):
    summed = jnp.zeros((padded.shape[0], height, breadth, padded.shape[3]), f32)
    for offset_row in range(7):
        for offset_col in range(7):
            window = padded[
                :, offset_row : offset_row + height, offset_col : offset_col + breadth, :
            ]
            summed = summed + window.astype(f32) * kernel[offset_row, offset_col].astype(f32)
    return summed


def kernel_terms(padded, grad_conv, height, breadth):
    grad_float = grad_conv.astype(f32)
    stacked = []
    for offset_row in range(7):
        for offset_col in range(7):
            window = padded[
                :, offset_row : offset_row + height, offset_col : offset_col + breadth, :
            ]
            stacked.append(jnp.sum(window.astype(f32) * grad_float, axis=(0, 1, 2)))
    return jnp.stack(stacked)


def gather_tokens(message):
    near = [message] + [fetch(message, "z_hi", 4, d) for d in (1, 2, 3)]
    near = jnp.concatenate(near, axis=1)
    ahead = fetch(near, "x", 4, 1)
    behind = fetch(near, "x", 4, 3)
    far = fetch(near, "x", 4, 2)
    return jnp.concatenate([near, ahead, far, behind], axis=1)


def scatter_sum(values):
    count = lax.axis_size(AXES)
    return lax.all_to_all(values.reshape(count, -1), AXES, 0, 0)


def gather_sum(parts):
    mine = jnp.sum(parts, axis=0, keepdims=True)
    return lax.all_to_all(jnp.broadcast_to(mine, parts.shape), AXES, 0, 0)


def params(name, megabytes):
    return dict(
        name=name, compiler_params=pltpu.CompilerParams(vmem_limit_bytes=megabytes << 20)
    )


def body(features, kernel, ln_gain, layer_scale, w_in, w_out, pairs, negatives):
    height, breadth, channels = (features.shape[1], features.shape[2], features.shape[3])
    pixels = height * breadth
    reg_rows, reg_cols = (height // REGION, breadth // REGION)
    tokens = reg_rows * reg_cols
    hidden_width = w_in.shape[1]
    z, x, y, core = (lax.axis_index(name) for name in ("z_hi", "x", "y", "core"))
    idx = jnp.stack([z, x, y, lax.axis_index("z_lo"), core]).astype(jnp.int32)

    rimmed = padded_rows(features, 3)
    padded = jnp.pad(rimmed, ((0, 0), (0, 0), (3, 3), (0, 0)))
    conv_rows = depthwise(padded, kernel, height, breadth).reshape(-1, channels)
    centred = conv_rows - jnp.mean(conv_rows, axis=-1, keepdims=True)
    spread = jnp.sqrt(jnp.mean(centred * centred, axis=-1, keepdims=True) + eps_layer)
    unit_rows = centred / spread
    normed = (unit_rows * ln_gain).astype(bf16)
    in_pieces, out_pieces, (normed, unit_rows, spread) = gather_weights(
        w_in, w_out, (normed, unit_rows, spread)
    )

    half = hidden_width // 2
    slope, pooled_hidden = pl.pallas_call(
        first_kernel,
        out_shape=(
            jax.ShapeDtypeStruct((2, pixels, half), f32),
            jax.ShapeDtypeStruct((2, 2 * tokens, half), bf16),
        ),
        in_specs=[SMEM, pl.BlockSpec()] + [ANY] * 10,
        scratch_shapes=[
            pltpu.VMEM((2, channels, half), bf16),
            pltpu.SemaphoreType.DMA((2,)),
        ],
        **params("expand_rows", 48),
    )(idx, normed, *in_pieces)

    width = channels // 2
    unit_tok, inv_norm, tokens_b = pl.pallas_call(
        second_kernel,
        out_shape=(
            jax.ShapeDtypeStruct((tokens, channels), f32),
            jax.ShapeDtypeStruct((tokens, 128), f32),
            jax.ShapeDtypeStruct((tokens, channels), bf16),
        ),
        in_specs=[SMEM] + [pl.BlockSpec()] * 3 + [ANY] * 10,
        scratch_shapes=[
            pltpu.VMEM((2, 4, 4, 4, hidden_width // 64, width), bf16),
            pltpu.VMEM((2, tokens, width), f32),
            pltpu.SemaphoreType.DMA((2,)),
        ],
        **params("pool_tokens", 32),
    )(
        idx,
        pooled_hidden,
        features.reshape(pixels, channels),
        layer_scale.reshape(1, channels),
        *out_pieces,
    )

    message = jnp.concatenate(
        [
            tokens_b.reshape(reg_rows, reg_cols, channels),
            jnp.pad(negatives[0].astype(bf16), ((0, 0), (0, 0), (0, 128 - NEG))),
        ],
        axis=2,
    )
    gathered = gather_tokens(message)
    keys = gathered[:, :, :channels]
    slot = jnp.arange(16, dtype=jnp.int32)
    image = ((z + slot % 4) % 4) * 4 + (x + slot // 4) % 4
    columns = jnp.arange(reg_cols, dtype=jnp.int32)
    ids = (image[:, None] * reg_cols + columns[None, :]).reshape(1, -1)
    positive = (pairs[image][:, None] * reg_cols + columns[None, :]).reshape(1, -1, 1)
    chosen = jnp.concatenate(
        [
            jnp.broadcast_to(positive, (reg_rows, positive.shape[1], 1)),
            gathered[:, :, channels : channels + NEG].astype(jnp.int32),
        ],
        axis=2,
    )

    grad_conv, scaled, loss_part = pl.pallas_call(
        third_kernel,
        out_shape=(
            jax.ShapeDtypeStruct((pixels, channels), bf16),
            jax.ShapeDtypeStruct((tokens, channels), f32),
            jax.ShapeDtypeStruct((1, 128), f32),
        ),
        in_specs=[SMEM] + [pl.BlockSpec()] * 8 + [ANY] * 22,
        scratch_shapes=[
            pltpu.VMEM((2, 4, 4, 4, hidden_width // 64, width), bf16),
            pltpu.VMEM((2, channels, half), bf16),
            pltpu.VMEM((2, pixels, half), f32),
            pltpu.VMEM((pixels, channels), f32),
            pltpu.VMEM((2, tokens, width), bf16),
            pltpu.VMEM((2, 3 * tokens, half), bf16),
            pltpu.VMEM((pixels, channels), f32),
            pltpu.SemaphoreType.DMA((2,)),
            pltpu.SemaphoreType.DMA((2,)),
            pltpu.SemaphoreType.DMA((2,)),
        ],
        **params("loss_and_back", 58),
    )(
        idx,
        keys,
        chosen,
        ids,
        unit_tok,
        inv_norm,
        layer_scale.reshape(1, channels),
        ln_gain.reshape(1, channels),
        jnp.broadcast_to(spread, (pixels, 128)),
        slope,
        unit_rows,
        *out_pieces,
        *in_pieces,
    )

    grad_conv = grad_conv.reshape(1, height, breadth, channels)
    kernel_local = kernel_terms(padded, grad_conv, height, breadth)
    loss_row = jnp.pad(loss_part[:, :1], ((0, 14), (0, channels - 1)))
    parts = scatter_sum(jnp.concatenate([kernel_local, loss_row], axis=0))

    grad_rim = padded_rows(grad_conv, 3)
    grad_pad = jnp.pad(grad_rim, ((0, 0), (0, 0), (3, 3), (0, 0)))
    conv_back = depthwise(grad_pad, kernel[::-1, ::-1], height, breadth)
    grad_out = jnp.broadcast_to(
        scaled.reshape(reg_rows, 1, reg_cols, 1, channels),
        (reg_rows, REGION, reg_cols, REGION, channels),
    ).reshape(1, height, breadth, channels)
    grad_features = (grad_out + conv_back).astype(bf16)
    parts, grad_features = lax.optimization_barrier((parts, grad_features))
    summed = gather_sum(parts).reshape(-1, channels)

    grad_kernel = summed[:49].reshape(7, 7, channels)
    token_count = lax.axis_size(AXES) * tokens
    loss = summed[49, 0] / float(token_count)
    return (grad_features, grad_kernel, loss)


def solution(mesh):
    split = Mesh(mesh.devices.reshape(4, 4, 4, 2, 2), AXES)
    return jax.shard_map(
        body,
        mesh=split,
        in_specs=(
            P(DP, ROWS, None, None),
            P(),
            P(),
            P(),
            P(AXES, None),
            P(AXES, None),
            P(),
            P(DP, ROWS, None, None),
        ),
        out_specs=(P(DP, ROWS, None, None), P(), P()),
        check_vma=False,
    )
```

```python
import jax
import jax.numpy as jnp
from jax import lax
from jax.experimental import pallas as pl
from jax.experimental.pallas import tpu as pltpu
from jax.sharding import Mesh, PartitionSpec as P

REGION = 4
NEG = 8
loss_scale = 1024.0
inv_temp = 16.0
eps_layer = 1e-06
eps_norm = 1e-06

AXES = ("z_hi", "x", "y", "z_lo", "core")
DP = ("z_hi", "x")
ROWS = ("y", "z_lo", "core")
bf16 = jnp.bfloat16
f32 = jnp.float32
ANY = pl.BlockSpec(memory_space=pl.ANY)
SMEM = pl.BlockSpec(memory_space=pltpu.SMEM)


def fetch(value, axis, count, distance):
    return lax.ppermute(value, axis, [((i + distance) % count, i) for i in range(count)])


def toward(value, axis, sign):
    pairs = []
    for i in range(4):
        for core in range(2):
            step = sign if core == 0 else -sign
            pairs.append((((i + step) % 4) * 2 + core, i * 2 + core))
    return lax.ppermute(value, (axis, "core"), pairs)


def ring(value, axis):
    near = toward(value, axis, 1)
    other = toward(value, axis, -1)
    return [value, near, other, toward(near, axis, 1)]


def distances(core):
    near = 1 + 2 * core
    return (0, near, 4 - near, 2)


def both_cores(pieces):
    return list(pieces) + [fetch(piece, "core", 2, 1) for piece in pieces]


def along_z(w_in, w_out):
    rows, width = w_in.shape[0], w_in.shape[1] // 2
    narrow = w_out.shape[1] // 2
    halves = [
        jnp.concatenate(
            [
                w_in[:, c * width : (c + 1) * width],
                w_out[:rows, c * narrow : (c + 1) * narrow],
                w_out[rows:, c * narrow : (c + 1) * narrow],
            ],
            axis=1,
        )
        for c in range(2)
    ]
    message = jnp.stack(halves)
    message = jnp.broadcast_to(message[None], (8,) + message.shape).reshape(16, rows, -1)
    got = lax.all_to_all(message, ("z_hi", "z_lo", "core"), 0, 0)
    near_in = got[:, :, :width].reshape(4, 4 * rows, width)
    near_out = jnp.concatenate(
        [got[:, :, width : width + narrow], got[:, :, width + narrow :]], axis=1
    ).reshape(4, 8 * rows, narrow)
    return near_in, near_out


def gather_weights(w_in, w_out, other_work):
    x, y = lax.axis_index("x"), lax.axis_index("y")
    far = distances(lax.axis_index("core"))
    near_in, near_out = along_z(w_in, w_out)
    near_in, near_out, other_work = lax.optimization_barrier((near_in, near_out, other_work))
    slot = jnp.arange(4).reshape(1, 4, 1, 1)
    parts_in = ring(near_in, "y")
    middle_in = parts_in[0][:, None]
    for piece, distance in zip(parts_in[1:], far[1:]):
        middle_in = jnp.where(slot == (y + distance) % 4, piece[:, None], middle_in)
    middle_in = middle_in.reshape(4, -1, near_in.shape[2])
    pieces_in = both_cores(ring(middle_in, "x"))
    parts_out = ring(near_out, "x")
    middle_out = parts_out[0][:, None]
    for piece, distance in zip(parts_out[1:], far[1:]):
        middle_out = jnp.where(slot == (x + distance) % 4, piece[:, None], middle_out)
    pieces_out = both_cores(ring(middle_out, "y"))
    return pieces_in, pieces_out, other_work


def copies_in(idx, pieces, held, sems):
    x = idx[1]
    for core in range(2):
        far = distances((idx[4] + core) % 2)
        for distance, piece in zip(far, pieces[core * 4 : core * 4 + 4]):
            rows = piece.shape[1]
            for i in range(piece.shape[0]):
                at = (i * 4 + (x + distance) % 4) * rows
                pltpu.make_async_copy(
                    piece.at[i],
                    held.at[core, pl.ds(pl.multiple_of(at, rows), rows), :],
                    sems.at[core],
                ).start()


def copies_out(idx, pieces, held, sems):
    y = idx[2]
    for core in range(2):
        far = distances((idx[4] + core) % 2)
        for distance, piece in zip(far, pieces[core * 4 : core * 4 + 4]):
            pltpu.make_async_copy(
                piece, held.at[core, :, :, (y + distance) % 4], sems.at[core]
            ).start()


def arrive(held, sems, core):
    pltpu.make_async_copy(held.at[core], held.at[core], sems.at[core]).wait()


def region_of(pixel):
    return ((pixel >> 7) << 3) + ((pixel & 31) >> 2)


def split2(value):
    high = value.astype(bf16)
    return high, (value - high.astype(f32)).astype(bf16)


def split3(value):
    high = value.astype(bf16)
    rest = value - high.astype(f32)
    mid = rest.astype(bf16)
    return high, mid, (rest - mid.astype(f32)).astype(bf16)


def pool_matrix(tokens, pixels):
    token = lax.broadcasted_iota(jnp.int32, (tokens, pixels), 0)
    pixel = lax.broadcasted_iota(jnp.int32, (tokens, pixels), 1)
    return jnp.where(region_of(pixel) == token, 1.0 / 16.0, 0.0).astype(bf16)


def dot(a, b):
    return jnp.dot(a, b, preferred_element_type=f32)


def dot_t(a, b):
    return lax.dot_general(a, b, (((1,), (1,)), ((), ())), preferred_element_type=f32)


def first_kernel(idx, normed, *refs):
    pieces, (slope, pooled, held, sems) = refs[:8], refs[8:]
    copies_in(idx, pieces, held, sems)
    pixels = normed.shape[0]
    tokens = pooled.shape[1] // 2
    steps = held.shape[2] // 512

    for core in range(2):
        arrive(held, sems, core)
        at = (idx[4] + core) % 2

        @pl.loop(0, steps)
        def _(step):
            lanes = pl.ds(pl.multiple_of(step * 512, 512), 512)
            pre = dot(normed[...], held[core, :, lanes])
            cdf = 0.5 * (1.0 + lax.erf(pre * 0.7071067811865476))
            density = jnp.exp(-0.5 * pre * pre) * 0.3989422804014327
            hidden = (pre * cdf).astype(bf16)
            slope[at, :, lanes] = cdf + pre * density
            high, low = split2(dot(pool_matrix(tokens, pixels), hidden))
            pooled[at, :tokens, lanes] = high
            pooled[at, tokens:, lanes] = low


def second_kernel(idx, hidden, feats, scale, *refs):
    pieces, (unit, norm, token, held, mixed, sems) = refs[:8], refs[8:]
    copies_out(idx, pieces, held, sems)
    tokens = unit.shape[0]
    base = dot(pool_matrix(tokens, feats.shape[0]), feats[...])
    half, width = hidden.shape[2], held.shape[5]
    for core in range(2):
        arrive(held, sems, core)
        at = (idx[4] + core) % 2
        low = held[core, :2].reshape(half, width)
        high = held[core, 2:].reshape(half, width)
        both = dot(hidden[0], low) + dot(hidden[1], high)
        mixed[at] = both[:tokens] + both[tokens:]
    full = jnp.concatenate([mixed[0], mixed[1]], axis=1)
    pool = base + scale[...] * full
    inv = lax.rsqrt(jnp.sum(pool * pool, axis=1, keepdims=True) + eps_norm)
    unit[...] = pool * inv
    norm[...] = jnp.broadcast_to(inv, norm.shape)
    token[...] = (pool * inv).astype(bf16)


def third_kernel(
    idx, keys, chosen, ids, unit, norm, scale, gain, spread, slope_hbm, rows_hbm, *refs
):
    out_pieces, in_pieces = refs[:8], refs[8:16]
    (grad_conv, scaled, loss, held_out, held_in, slope, rows, mix, hid, total_ref) = refs[16:26]
    sem_out, sem_in, sem = refs[26:]
    copies_out(idx, out_pieces, held_out, sem_out)
    copies_in(idx, in_pieces, held_in, sem_in)
    copy_slope = pltpu.make_async_copy(slope_hbm, slope, sem.at[0])
    copy_slope.start()
    copy_rows = pltpu.make_async_copy(rows_hbm, rows, sem.at[1])
    copy_rows.start()
    token_grads, losses = [], []
    for r in range(keys.shape[0]):
        key = keys[r]
        count = key.shape[0]
        similar = dot_t(key, key)
        hits, logits = [], []
        for n in range(NEG + 1):
            hit = chosen[r, :, n : n + 1] == ids[...]
            hits.append(hit)
            logits.append(
                inv_temp * jnp.sum(jnp.where(hit, similar, 0.0), axis=1, keepdims=True)
            )
        exps = [jnp.exp(value) for value in logits]
        total = exps[0]
        for value in exps[1:]:
            total = total + value
        weight = jnp.zeros((count, count), f32)
        for n in range(NEG + 1):
            coef = loss_scale * inv_temp * (exps[n] / total - (1.0 if n == 0 else 0.0))
            weight = weight + jnp.where(hits[n], coef, 0.0)
        own = weight[:8] + jnp.transpose(weight)[:8]
        high, mid, low = split3(own)
        token_grads.append(dot(high, key) + dot(mid, key) + dot(low, key))
        losses.append((jnp.log(total) - logits[0])[:8])
    loss[...] = jnp.broadcast_to(
        jnp.sum(losses[0] + losses[1], axis=0, keepdims=True), loss.shape
    )
    grad_tok = jnp.concatenate(token_grads, axis=0)
    unit_v = unit[...]
    grad_pool = (grad_tok - unit_v * jnp.sum(unit_v * grad_tok, axis=1, keepdims=True)) * norm[
        :, :1
    ]
    spread_grad = grad_pool / 16.0
    scaled[...] = spread_grad
    grad_mix = (scale[...] * spread_grad).astype(bf16)
    width = held_out.shape[5]
    mix[0] = grad_mix[:, :width]
    mix[1] = grad_mix[:, width:]
    part = None
    for core in range(2):
        arrive(held_out, sem_out, core)
        at = (idx[4] + core) % 2
        term = dot_t(held_out[core].reshape(-1, width), mix[at])
        part = term if part is None else part + term
    half = held_in.shape[2]
    tokens = part.shape[1]
    for k in range(2):
        for i, piece in enumerate(split3(jnp.transpose(part[k * half : (k + 1) * half]))):
            hid[k, i * tokens : (i + 1) * tokens] = piece
    copy_slope.wait()
    pixels = rows.shape[0]
    total_ref[...] = jnp.zeros(total_ref.shape, f32)
    for core in range(2):
        arrive(held_in, sem_in, core)
        at = (idx[4] + core) % 2

        @pl.loop(0, half // 512)
        def _(step):
            lanes = pl.ds(pl.multiple_of(step * 512, 512), 512)
            pixel = lax.broadcasted_iota(jnp.int32, (pixels, 3 * tokens), 0)
            token = lax.broadcasted_iota(jnp.int32, (pixels, 3 * tokens), 1) & (tokens - 1)
            expand = jnp.where(region_of(pixel) == token, 1.0, 0.0).astype(bf16)
            wide = dot(expand, hid[at, :, lanes])
            grad_pre = (wide * slope[at, :, lanes]).astype(bf16)
            total_ref[...] += dot_t(grad_pre, held_in[core, :, lanes])

    copy_rows.wait()
    grad_unit = total_ref[...] * gain[...]
    unit_rows = rows[...]
    mean_one = jnp.mean(grad_unit, axis=1, keepdims=True)
    mean_two = jnp.mean(grad_unit * unit_rows, axis=1, keepdims=True)
    grad_conv[...] = ((grad_unit - mean_one - unit_rows * mean_two) / spread[:, :1]).astype(bf16)


def padded_rows(cells, width):
    count = lax.axis_size(ROWS)
    ends = count - 1
    head = cells[:, :width]
    tail = cells[:, cells.shape[1] - width :]
    return jnp.concatenate(
        [
            lax.ppermute(tail, ROWS, [(i, i + 1) for i in range(ends)]),
            cells,
            lax.ppermute(head, ROWS, [(i + 1, i) for i in range(ends)]),
        ],
        axis=1,
    )


def depthwise(padded, kernel, height, breadth):
    summed = jnp.zeros((padded.shape[0], height, breadth, padded.shape[3]), f32)
    for offset_row in range(7):
        for offset_col in range(7):
            window = padded[
                :, offset_row : offset_row + height, offset_col : offset_col + breadth, :
            ]
            summed = summed + window.astype(f32) * kernel[offset_row, offset_col].astype(f32)
    return summed


def kernel_terms(padded, grad_conv, height, breadth):
    grad_float = grad_conv.astype(f32)
    stacked = []
    for offset_row in range(7):
        for offset_col in range(7):
            window = padded[
                :, offset_row : offset_row + height, offset_col : offset_col + breadth, :
            ]
            stacked.append(jnp.sum(window.astype(f32) * grad_float, axis=(0, 1, 2)))
    return jnp.stack(stacked)


def gather_tokens(message):
    near = [message] + [fetch(message, "z_hi", 4, d) for d in (1, 2, 3)]
    near = jnp.concatenate(near, axis=1)
    ahead = fetch(near, "x", 4, 1)
    behind = fetch(near, "x", 4, 3)
    far = fetch(near, "x", 4, 2)
    return jnp.concatenate([near, ahead, far, behind], axis=1)


def spread_over(value, axes):
    count = lax.axis_size(axes)
    return lax.all_to_all(jnp.broadcast_to(value[None], (count,) + value.shape), axes, 0, 0)


def own_first(own, other):
    first = lax.axis_index("core") == 0
    return jnp.where(
        first, jnp.concatenate([own, other], axis=1), jnp.concatenate([other, own], axis=1)
    )


def total_over_all(values):
    width = values.shape[1] // 2
    first = lax.axis_index("core") == 0
    left, right = values[:, :width], values[:, width:]
    part = jnp.where(first, left, right) + fetch(jnp.where(first, right, left), "core", 2, 1)
    part = lax.all_to_all(part.reshape(16, -1, width), ("x", "y"), 0, 0)
    part = jnp.sum(part, axis=0)
    part = jnp.sum(spread_over(part, ("z_hi", "z_lo")), axis=0)
    part = spread_over(part, ("x", "y")).reshape(-1, width)
    return own_first(part, fetch(part, "core", 2, 1))


def params(name, megabytes):
    return dict(
        name=name, compiler_params=pltpu.CompilerParams(vmem_limit_bytes=megabytes << 20)
    )


def body(features, kernel, ln_gain, layer_scale, w_in, w_out, pairs, negatives):
    height, breadth, channels = (features.shape[1], features.shape[2], features.shape[3])
    pixels = height * breadth
    reg_rows, reg_cols = (height // REGION, breadth // REGION)
    tokens = reg_rows * reg_cols
    hidden_width = w_in.shape[1]
    z, x, y, core = (lax.axis_index(name) for name in ("z_hi", "x", "y", "core"))
    idx = jnp.stack([z, x, y, lax.axis_index("z_lo"), core]).astype(jnp.int32)

    rimmed = padded_rows(features, 3)
    padded = jnp.pad(rimmed, ((0, 0), (0, 0), (3, 3), (0, 0)))
    conv_rows = depthwise(padded, kernel, height, breadth).reshape(-1, channels)
    in_pieces, out_pieces, conv_rows = gather_weights(w_in, w_out, conv_rows)
    centred = conv_rows - jnp.mean(conv_rows, axis=-1, keepdims=True)
    spread = jnp.sqrt(jnp.mean(centred * centred, axis=-1, keepdims=True) + eps_layer)
    unit_rows = centred / spread
    normed = (unit_rows * ln_gain).astype(bf16)

    half = hidden_width // 2
    slope, pooled_hidden = pl.pallas_call(
        first_kernel,
        out_shape=(
            jax.ShapeDtypeStruct((2, pixels, half), f32),
            jax.ShapeDtypeStruct((2, 2 * tokens, half), bf16),
        ),
        in_specs=[SMEM, pl.BlockSpec()] + [ANY] * 8,
        scratch_shapes=[
            pltpu.VMEM((2, channels, half), bf16),
            pltpu.SemaphoreType.DMA((2,)),
        ],
        **params("expand_rows", 48),
    )(idx, normed, *in_pieces)

    width = channels // 2
    unit_tok, inv_norm, tokens_b = pl.pallas_call(
        second_kernel,
        out_shape=(
            jax.ShapeDtypeStruct((tokens, channels), f32),
            jax.ShapeDtypeStruct((tokens, 128), f32),
            jax.ShapeDtypeStruct((tokens, channels), bf16),
        ),
        in_specs=[SMEM] + [pl.BlockSpec()] * 3 + [ANY] * 8,
        scratch_shapes=[
            pltpu.VMEM((2, 4, 4, 4, hidden_width // 64, width), bf16),
            pltpu.VMEM((2, tokens, width), f32),
            pltpu.SemaphoreType.DMA((2,)),
        ],
        **params("pool_tokens", 32),
    )(
        idx,
        pooled_hidden,
        features.reshape(pixels, channels),
        layer_scale.reshape(1, channels),
        *out_pieces,
    )

    message = jnp.concatenate(
        [
            tokens_b.reshape(reg_rows, reg_cols, channels),
            jnp.pad(negatives[0].astype(bf16), ((0, 0), (0, 0), (0, 128 - NEG))),
        ],
        axis=2,
    )
    gathered = gather_tokens(message)
    keys = gathered[:, :, :channels]
    slot = jnp.arange(16, dtype=jnp.int32)
    image = ((z + slot % 4) % 4) * 4 + (x + slot // 4) % 4
    columns = jnp.arange(reg_cols, dtype=jnp.int32)
    ids = (image[:, None] * reg_cols + columns[None, :]).reshape(1, -1)
    positive = (pairs[image][:, None] * reg_cols + columns[None, :]).reshape(1, -1, 1)
    chosen = jnp.concatenate(
        [
            jnp.broadcast_to(positive, (reg_rows, positive.shape[1], 1)),
            gathered[:, :, channels : channels + NEG].astype(jnp.int32),
        ],
        axis=2,
    )

    grad_conv, scaled, loss_part = pl.pallas_call(
        third_kernel,
        out_shape=(
            jax.ShapeDtypeStruct((pixels, channels), bf16),
            jax.ShapeDtypeStruct((tokens, channels), f32),
            jax.ShapeDtypeStruct((1, 128), f32),
        ),
        in_specs=[SMEM] + [pl.BlockSpec()] * 8 + [ANY] * 18,
        scratch_shapes=[
            pltpu.VMEM((2, 4, 4, 4, hidden_width // 64, width), bf16),
            pltpu.VMEM((2, channels, half), bf16),
            pltpu.VMEM((2, pixels, half), f32),
            pltpu.VMEM((pixels, channels), f32),
            pltpu.VMEM((2, tokens, width), bf16),
            pltpu.VMEM((2, 3 * tokens, half), bf16),
            pltpu.VMEM((pixels, channels), f32),
            pltpu.SemaphoreType.DMA((2,)),
            pltpu.SemaphoreType.DMA((2,)),
            pltpu.SemaphoreType.DMA((2,)),
        ],
        **params("loss_and_back", 58),
    )(
        idx,
        keys,
        chosen,
        ids,
        unit_tok,
        inv_norm,
        layer_scale.reshape(1, channels),
        ln_gain.reshape(1, channels),
        jnp.broadcast_to(spread, (pixels, 128)),
        slope,
        unit_rows,
        *out_pieces,
        *in_pieces,
    )

    grad_conv = grad_conv.reshape(1, height, breadth, channels)
    kernel_local = kernel_terms(padded, grad_conv, height, breadth)
    loss_row = jnp.pad(loss_part[:, :1], ((0, 14), (0, channels - 1)))
    summed = total_over_all(jnp.concatenate([kernel_local, loss_row], axis=0))

    grad_rim = padded_rows(grad_conv, 3)
    grad_pad = jnp.pad(grad_rim, ((0, 0), (0, 0), (3, 3), (0, 0)))
    conv_back = depthwise(grad_pad, kernel[::-1, ::-1], height, breadth)
    grad_out = jnp.broadcast_to(
        scaled.reshape(reg_rows, 1, reg_cols, 1, channels),
        (reg_rows, REGION, reg_cols, REGION, channels),
    ).reshape(1, height, breadth, channels)
    grad_features = (grad_out + conv_back).astype(bf16)

    grad_kernel = summed[:49].reshape(7, 7, channels)
    token_count = lax.axis_size(AXES) * tokens
    loss = summed[49, 0] / float(token_count)
    return (grad_features, grad_kernel, loss)


def solution(mesh):
    split = Mesh(mesh.devices.reshape(4, 4, 4, 2, 2), AXES)
    return jax.shard_map(
        body,
        mesh=split,
        in_specs=(
            P(DP, ROWS, None, None),
            P(),
            P(),
            P(),
            P(AXES, None),
            P(AXES, None),
            P(),
            P(DP, ROWS, None, None),
        ),
        out_specs=(P(DP, ROWS, None, None), P(), P()),
        check_vma=False,
    )
```

```python
import jax
import jax.numpy as jnp
from jax import lax
from jax.experimental import pallas as pl
from jax.experimental.pallas import tpu as pltpu
from jax.sharding import Mesh, PartitionSpec as P

REGION = 4
NEG = 8
loss_scale = 1024.0
inv_temp = 16.0
eps_layer = 1e-06
eps_norm = 1e-06

AXES = ("z_hi", "x", "y", "z_lo", "core")
DP = ("z_hi", "x")
ROWS = ("y", "z_lo", "core")
bf16 = jnp.bfloat16
f32 = jnp.float32
ANY = pl.BlockSpec(memory_space=pl.ANY)
SMEM = pl.BlockSpec(memory_space=pltpu.SMEM)


def fetch(value, axis, count, distance):
    return lax.ppermute(value, axis, [((i + distance) % count, i) for i in range(count)])


def toward(value, axis, sign):
    pairs = []
    for i in range(4):
        for core in range(2):
            step = sign if core == 0 else -sign
            pairs.append((((i + step) % 4) * 2 + core, i * 2 + core))
    return lax.ppermute(value, (axis, "core"), pairs)


def ring(value, axis, later=()):
    near = toward(value, axis, 1)
    value, near, later = lax.optimization_barrier((value, near, later))
    pieces = [value, near, toward(value, axis, -1), toward(near, axis, 1)]
    return pieces if isinstance(later, tuple) else (pieces, later)


def placed(pieces, position, dim):
    shape = [1] * (pieces[0].ndim + 1)
    shape[dim] = 4
    slot = jnp.arange(4).reshape(shape)
    whole = jnp.expand_dims(pieces[0], dim)
    for piece, distance in zip(pieces[1:], distances(lax.axis_index("core"))[1:]):
        whole = jnp.where(slot == (position + distance) % 4, jnp.expand_dims(piece, dim), whole)
    return whole


def distances(core):
    near = 1 + 2 * core
    return (0, near, 4 - near, 2)


def both_cores(pieces):
    return list(pieces) + [fetch(piece, "core", 2, 1) for piece in pieces]


def along_z(w_in, w_out):
    rows, width = w_in.shape[0], w_in.shape[1] // 2
    narrow = w_out.shape[1] // 2
    halves = [
        jnp.concatenate(
            [
                w_in[:, c * width : (c + 1) * width],
                w_out[:rows, c * narrow : (c + 1) * narrow],
                w_out[rows:, c * narrow : (c + 1) * narrow],
            ],
            axis=1,
        )
        for c in range(2)
    ]
    low_core, low_z = lax.axis_index("core") == 0, lax.axis_index("z_lo") == 0
    keep = jnp.where(low_core, halves[0], halves[1])
    got = fetch(jnp.where(low_core, halves[1], halves[0]), "core", 2, 1)
    pair = jnp.where(low_core, jnp.stack([keep, got]), jnp.stack([got, keep]))
    got = fetch(pair, "z_lo", 2, 1)
    quad = jnp.where(low_z, jnp.concatenate([pair, got]), jnp.concatenate([got, pair]))
    got = placed(ring(quad, "z_hi"), lax.axis_index("z_hi"), 0).reshape(16, rows, -1)
    near_in = got[:, :, :width].reshape(4, 4 * rows, width)
    near_out = jnp.concatenate(
        [got[:, :, width : width + narrow], got[:, :, width + narrow :]], axis=1
    ).reshape(4, 8 * rows, narrow)
    return near_in, near_out


def gather_weights(w_in, w_out, later):
    near_in, near_out = along_z(w_in, w_out)
    middle_in = placed(ring(near_in, "y"), lax.axis_index("y"), 1)
    middle_in = middle_in.reshape(4, -1, near_in.shape[2])
    middle_out = placed(ring(near_out, "x"), lax.axis_index("x"), 1)
    pieces_in, later = ring(middle_in, "x", later)
    pieces_out = ring(middle_out, "y")
    return both_cores(pieces_in), both_cores(pieces_out), later


def copies_in(idx, pieces, held, sems):
    x = idx[1]
    for core in range(2):
        far = distances((idx[4] + core) % 2)
        for distance, piece in zip(far, pieces[core * 4 : core * 4 + 4]):
            rows = piece.shape[1]
            for i in range(piece.shape[0]):
                at = (i * 4 + (x + distance) % 4) * rows
                pltpu.make_async_copy(
                    piece.at[i],
                    held.at[core, pl.ds(pl.multiple_of(at, rows), rows), :],
                    sems.at[core],
                ).start()


def copies_out(idx, pieces, held, sems):
    y = idx[2]
    for core in range(2):
        far = distances((idx[4] + core) % 2)
        for distance, piece in zip(far, pieces[core * 4 : core * 4 + 4]):
            pltpu.make_async_copy(
                piece, held.at[core, :, :, (y + distance) % 4], sems.at[core]
            ).start()


def arrive(held, sems, core):
    pltpu.make_async_copy(held.at[core], held.at[core], sems.at[core]).wait()


def region_of(pixel):
    return ((pixel >> 7) << 3) + ((pixel & 31) >> 2)


def split2(value):
    high = value.astype(bf16)
    return high, (value - high.astype(f32)).astype(bf16)


def split3(value):
    high = value.astype(bf16)
    rest = value - high.astype(f32)
    mid = rest.astype(bf16)
    return high, mid, (rest - mid.astype(f32)).astype(bf16)


def pool_matrix(tokens, pixels):
    token = lax.broadcasted_iota(jnp.int32, (tokens, pixels), 0)
    pixel = lax.broadcasted_iota(jnp.int32, (tokens, pixels), 1)
    return jnp.where(region_of(pixel) == token, 1.0 / 16.0, 0.0).astype(bf16)


def dot(a, b):
    return jnp.dot(a, b, preferred_element_type=f32)


def dot_t(a, b):
    return lax.dot_general(a, b, (((1,), (1,)), ((), ())), preferred_element_type=f32)


def first_kernel(idx, normed, *refs):
    pieces, (slope, pooled, held, sems) = refs[:8], refs[8:]
    copies_in(idx, pieces, held, sems)
    pixels = normed.shape[0]
    tokens = pooled.shape[1] // 2
    steps = held.shape[2] // 512

    for core in range(2):
        arrive(held, sems, core)
        at = (idx[4] + core) % 2

        @pl.loop(0, steps)
        def _(step):
            lanes = pl.ds(pl.multiple_of(step * 512, 512), 512)
            pre = dot(normed[...], held[core, :, lanes])
            cdf = 0.5 * (1.0 + lax.erf(pre * 0.7071067811865476))
            density = jnp.exp(-0.5 * pre * pre) * 0.3989422804014327
            hidden = (pre * cdf).astype(bf16)
            slope[at, :, lanes] = cdf + pre * density
            high, low = split2(dot(pool_matrix(tokens, pixels), hidden))
            pooled[at, :tokens, lanes] = high
            pooled[at, tokens:, lanes] = low


def second_kernel(idx, hidden, feats, scale, *refs):
    pieces, (unit, norm, token, held, mixed, sems) = refs[:8], refs[8:]
    copies_out(idx, pieces, held, sems)
    tokens = unit.shape[0]
    base = dot(pool_matrix(tokens, feats.shape[0]), feats[...])
    half, width = hidden.shape[2], held.shape[5]
    for core in range(2):
        arrive(held, sems, core)
        at = (idx[4] + core) % 2
        low = held[core, :2].reshape(half, width)
        high = held[core, 2:].reshape(half, width)
        both = dot(hidden[0], low) + dot(hidden[1], high)
        mixed[at] = both[:tokens] + both[tokens:]
    full = jnp.concatenate([mixed[0], mixed[1]], axis=1)
    pool = base + scale[...] * full
    inv = lax.rsqrt(jnp.sum(pool * pool, axis=1, keepdims=True) + eps_norm)
    unit[...] = pool * inv
    norm[...] = jnp.broadcast_to(inv, norm.shape)
    token[...] = (pool * inv).astype(bf16)


def third_kernel(
    idx, keys, chosen, ids, unit, norm, scale, gain, spread, slope_hbm, rows_hbm, *refs
):
    out_pieces, in_pieces = refs[:8], refs[8:16]
    (grad_conv, scaled, loss, held_out, held_in, slope, rows, mix, hid, total_ref) = refs[16:26]
    sem_out, sem_in, sem = refs[26:]
    copies_out(idx, out_pieces, held_out, sem_out)
    copies_in(idx, in_pieces, held_in, sem_in)
    copy_slope = pltpu.make_async_copy(slope_hbm, slope, sem.at[0])
    copy_slope.start()
    copy_rows = pltpu.make_async_copy(rows_hbm, rows, sem.at[1])
    copy_rows.start()
    token_grads, losses = [], []
    for r in range(keys.shape[0]):
        key = keys[r]
        count = key.shape[0]
        similar = dot_t(key, key)
        hits, logits = [], []
        for n in range(NEG + 1):
            hit = chosen[r, :, n : n + 1] == ids[...]
            hits.append(hit)
            logits.append(
                inv_temp * jnp.sum(jnp.where(hit, similar, 0.0), axis=1, keepdims=True)
            )
        exps = [jnp.exp(value) for value in logits]
        total = exps[0]
        for value in exps[1:]:
            total = total + value
        weight = jnp.zeros((count, count), f32)
        for n in range(NEG + 1):
            coef = loss_scale * inv_temp * (exps[n] / total - (1.0 if n == 0 else 0.0))
            weight = weight + jnp.where(hits[n], coef, 0.0)
        own = weight[:8] + jnp.transpose(weight)[:8]
        high, mid, low = split3(own)
        token_grads.append(dot(high, key) + dot(mid, key) + dot(low, key))
        losses.append((jnp.log(total) - logits[0])[:8])
    loss[...] = jnp.broadcast_to(
        jnp.sum(losses[0] + losses[1], axis=0, keepdims=True), loss.shape
    )
    grad_tok = jnp.concatenate(token_grads, axis=0)
    unit_v = unit[...]
    grad_pool = (grad_tok - unit_v * jnp.sum(unit_v * grad_tok, axis=1, keepdims=True)) * norm[
        :, :1
    ]
    spread_grad = grad_pool / 16.0
    scaled[...] = spread_grad
    grad_mix = (scale[...] * spread_grad).astype(bf16)
    width = held_out.shape[5]
    mix[0] = grad_mix[:, :width]
    mix[1] = grad_mix[:, width:]
    part = None
    for core in range(2):
        arrive(held_out, sem_out, core)
        at = (idx[4] + core) % 2
        term = dot_t(held_out[core].reshape(-1, width), mix[at])
        part = term if part is None else part + term
    half = held_in.shape[2]
    tokens = part.shape[1]
    for k in range(2):
        for i, piece in enumerate(split3(jnp.transpose(part[k * half : (k + 1) * half]))):
            hid[k, i * tokens : (i + 1) * tokens] = piece
    copy_slope.wait()
    pixels = rows.shape[0]
    total_ref[...] = jnp.zeros(total_ref.shape, f32)
    for core in range(2):
        arrive(held_in, sem_in, core)
        at = (idx[4] + core) % 2

        @pl.loop(0, half // 512)
        def _(step):
            lanes = pl.ds(pl.multiple_of(step * 512, 512), 512)
            pixel = lax.broadcasted_iota(jnp.int32, (pixels, 3 * tokens), 0)
            token = lax.broadcasted_iota(jnp.int32, (pixels, 3 * tokens), 1) & (tokens - 1)
            expand = jnp.where(region_of(pixel) == token, 1.0, 0.0).astype(bf16)
            wide = dot(expand, hid[at, :, lanes])
            grad_pre = (wide * slope[at, :, lanes]).astype(bf16)
            total_ref[...] += dot_t(grad_pre, held_in[core, :, lanes])

    copy_rows.wait()
    grad_unit = total_ref[...] * gain[...]
    unit_rows = rows[...]
    mean_one = jnp.mean(grad_unit, axis=1, keepdims=True)
    mean_two = jnp.mean(grad_unit * unit_rows, axis=1, keepdims=True)
    grad_conv[...] = ((grad_unit - mean_one - unit_rows * mean_two) / spread[:, :1]).astype(bf16)


def padded_rows(cells, width):
    count = lax.axis_size(ROWS)
    ends = count - 1
    head = cells[:, :width]
    tail = cells[:, cells.shape[1] - width :]
    return jnp.concatenate(
        [
            lax.ppermute(tail, ROWS, [(i, i + 1) for i in range(ends)]),
            cells,
            lax.ppermute(head, ROWS, [(i + 1, i) for i in range(ends)]),
        ],
        axis=1,
    )


def depthwise(padded, kernel, height, breadth):
    summed = jnp.zeros((padded.shape[0], height, breadth, padded.shape[3]), f32)
    for offset_row in range(7):
        for offset_col in range(7):
            window = padded[
                :, offset_row : offset_row + height, offset_col : offset_col + breadth, :
            ]
            summed = summed + window.astype(f32) * kernel[offset_row, offset_col].astype(f32)
    return summed


def kernel_terms(padded, grad_conv, height, breadth):
    grad_float = grad_conv.astype(f32)
    stacked = []
    for offset_row in range(7):
        for offset_col in range(7):
            window = padded[
                :, offset_row : offset_row + height, offset_col : offset_col + breadth, :
            ]
            stacked.append(jnp.sum(window.astype(f32) * grad_float, axis=(0, 1, 2)))
    return jnp.stack(stacked)


def gather_tokens(message):
    near = [message] + [fetch(message, "z_hi", 4, d) for d in (1, 2, 3)]
    near = jnp.concatenate(near, axis=1)
    ahead = fetch(near, "x", 4, 1)
    behind = fetch(near, "x", 4, 3)
    far = fetch(near, "x", 4, 2)
    return jnp.concatenate([near, ahead, far, behind], axis=1)


def spread_over(value, axes):
    count = lax.axis_size(axes)
    return lax.all_to_all(jnp.broadcast_to(value[None], (count,) + value.shape), axes, 0, 0)


def own_first(own, other):
    first = lax.axis_index("core") == 0
    return jnp.where(
        first, jnp.concatenate([own, other], axis=1), jnp.concatenate([other, own], axis=1)
    )


def total_over_all(values, work):
    width = values.shape[1] // 2
    first = lax.axis_index("core") == 0
    left, right = values[:, :width], values[:, width:]
    part = jnp.where(first, left, right) + fetch(jnp.where(first, right, left), "core", 2, 1)
    part = lax.all_to_all(part.reshape(16, -1, width), ("x", "y"), 0, 0)
    done = [work[0]()]
    part, done[0] = lax.optimization_barrier((part, done[0]))
    part = spread_over(jnp.sum(part, axis=0), ("z_hi", "z_lo"))
    done.append(work[1]())
    part, done[1] = lax.optimization_barrier((part, done[1]))
    part = spread_over(jnp.sum(part, axis=0), ("x", "y"))
    done.append(work[2]())
    part, done[2] = lax.optimization_barrier((part, done[2]))
    part = part.reshape(-1, width)
    return own_first(part, fetch(part, "core", 2, 1)), done


def params(name, megabytes):
    return dict(
        name=name, compiler_params=pltpu.CompilerParams(vmem_limit_bytes=megabytes << 20)
    )


def body(features, kernel, ln_gain, layer_scale, w_in, w_out, pairs, negatives):
    height, breadth, channels = (features.shape[1], features.shape[2], features.shape[3])
    pixels = height * breadth
    reg_rows, reg_cols = (height // REGION, breadth // REGION)
    tokens = reg_rows * reg_cols
    hidden_width = w_in.shape[1]
    z, x, y, core = (lax.axis_index(name) for name in ("z_hi", "x", "y", "core"))
    idx = jnp.stack([z, x, y, lax.axis_index("z_lo"), core]).astype(jnp.int32)

    rimmed = padded_rows(features, 3)
    in_pieces, out_pieces, rimmed = gather_weights(w_in, w_out, rimmed)
    padded = jnp.pad(rimmed, ((0, 0), (0, 0), (3, 3), (0, 0)))
    conv_rows = depthwise(padded, kernel, height, breadth).reshape(-1, channels)
    centred = conv_rows - jnp.mean(conv_rows, axis=-1, keepdims=True)
    spread = jnp.sqrt(jnp.mean(centred * centred, axis=-1, keepdims=True) + eps_layer)
    unit_rows = centred / spread
    normed = (unit_rows * ln_gain).astype(bf16)

    half = hidden_width // 2
    slope, pooled_hidden = pl.pallas_call(
        first_kernel,
        out_shape=(
            jax.ShapeDtypeStruct((2, pixels, half), f32),
            jax.ShapeDtypeStruct((2, 2 * tokens, half), bf16),
        ),
        in_specs=[SMEM, pl.BlockSpec()] + [ANY] * 8,
        scratch_shapes=[
            pltpu.VMEM((2, channels, half), bf16),
            pltpu.SemaphoreType.DMA((2,)),
        ],
        **params("expand_rows", 48),
    )(idx, normed, *in_pieces)

    width = channels // 2
    unit_tok, inv_norm, tokens_b = pl.pallas_call(
        second_kernel,
        out_shape=(
            jax.ShapeDtypeStruct((tokens, channels), f32),
            jax.ShapeDtypeStruct((tokens, 128), f32),
            jax.ShapeDtypeStruct((tokens, channels), bf16),
        ),
        in_specs=[SMEM] + [pl.BlockSpec()] * 3 + [ANY] * 8,
        scratch_shapes=[
            pltpu.VMEM((2, 4, 4, 4, hidden_width // 64, width), bf16),
            pltpu.VMEM((2, tokens, width), f32),
            pltpu.SemaphoreType.DMA((2,)),
        ],
        **params("pool_tokens", 32),
    )(
        idx,
        pooled_hidden,
        features.reshape(pixels, channels),
        layer_scale.reshape(1, channels),
        *out_pieces,
    )

    message = jnp.concatenate(
        [
            tokens_b.reshape(reg_rows, reg_cols, channels),
            jnp.pad(negatives[0].astype(bf16), ((0, 0), (0, 0), (0, 128 - NEG))),
        ],
        axis=2,
    )
    gathered = gather_tokens(message)
    keys = gathered[:, :, :channels]
    slot = jnp.arange(16, dtype=jnp.int32)
    image = ((z + slot % 4) % 4) * 4 + (x + slot // 4) % 4
    columns = jnp.arange(reg_cols, dtype=jnp.int32)
    ids = (image[:, None] * reg_cols + columns[None, :]).reshape(1, -1)
    positive = (pairs[image][:, None] * reg_cols + columns[None, :]).reshape(1, -1, 1)
    chosen = jnp.concatenate(
        [
            jnp.broadcast_to(positive, (reg_rows, positive.shape[1], 1)),
            gathered[:, :, channels : channels + NEG].astype(jnp.int32),
        ],
        axis=2,
    )

    grad_conv, scaled, loss_part = pl.pallas_call(
        third_kernel,
        out_shape=(
            jax.ShapeDtypeStruct((pixels, channels), bf16),
            jax.ShapeDtypeStruct((tokens, channels), f32),
            jax.ShapeDtypeStruct((1, 128), f32),
        ),
        in_specs=[SMEM] + [pl.BlockSpec()] * 8 + [ANY] * 18,
        scratch_shapes=[
            pltpu.VMEM((2, 4, 4, 4, hidden_width // 64, width), bf16),
            pltpu.VMEM((2, channels, half), bf16),
            pltpu.VMEM((2, pixels, half), f32),
            pltpu.VMEM((pixels, channels), f32),
            pltpu.VMEM((2, tokens, width), bf16),
            pltpu.VMEM((2, 3 * tokens, half), bf16),
            pltpu.VMEM((pixels, channels), f32),
            pltpu.SemaphoreType.DMA((2,)),
            pltpu.SemaphoreType.DMA((2,)),
            pltpu.SemaphoreType.DMA((2,)),
        ],
        **params("loss_and_back", 58),
    )(
        idx,
        keys,
        chosen,
        ids,
        unit_tok,
        inv_norm,
        layer_scale.reshape(1, channels),
        ln_gain.reshape(1, channels),
        jnp.broadcast_to(spread, (pixels, 128)),
        slope,
        unit_rows,
        *out_pieces,
        *in_pieces,
    )

    grad_conv = grad_conv.reshape(1, height, breadth, channels)
    kernel_local = kernel_terms(padded, grad_conv, height, breadth)
    loss_row = jnp.pad(loss_part[:, :1], ((0, 14), (0, channels - 1)))
    local = jnp.concatenate([kernel_local, loss_row], axis=0)
    grad_rim, local = lax.optimization_barrier((padded_rows(grad_conv, 3), local))
    grad_pad = jnp.pad(grad_rim, ((0, 0), (0, 0), (3, 3), (0, 0)))
    flipped = kernel[::-1, ::-1]
    third = channels // 3

    def back(k):
        lanes = slice(k * third, (k + 1) * third)
        conv_back = depthwise(grad_pad[..., lanes], flipped[..., lanes], height, breadth)
        grad_out = jnp.broadcast_to(
            scaled[:, lanes].reshape(reg_rows, 1, reg_cols, 1, third),
            (reg_rows, REGION, reg_cols, REGION, third),
        ).reshape(1, height, breadth, third)
        return (grad_out + conv_back).astype(bf16)

    summed, backs = total_over_all(local, [lambda k=k: back(k) for k in range(3)])
    grad_features = jnp.concatenate(backs, axis=3)

    grad_kernel = summed[:49].reshape(7, 7, channels)
    token_count = lax.axis_size(AXES) * tokens
    loss = summed[49, 0] / float(token_count)
    return (grad_features, grad_kernel, loss)


def solution(mesh):
    split = Mesh(mesh.devices.reshape(4, 4, 4, 2, 2), AXES)
    return jax.shard_map(
        body,
        mesh=split,
        in_specs=(
            P(DP, ROWS, None, None),
            P(),
            P(),
            P(),
            P(AXES, None),
            P(AXES, None),
            P(),
            P(DP, ROWS, None, None),
        ),
        out_specs=(P(DP, ROWS, None, None), P(), P()),
        check_vma=False,
    )
```

```python
import jax
import jax.numpy as jnp
from jax import lax
from jax.experimental import pallas as pl
from jax.experimental.pallas import tpu as pltpu
from jax.sharding import Mesh, PartitionSpec as P

REGION = 4
NEG = 8
loss_scale = 1024.0
inv_temp = 16.0
eps_layer = 1e-06
eps_norm = 1e-06

AXES = ("z_hi", "x", "y", "z_lo", "core")
DP = ("z_hi", "x")
ROWS = ("y", "z_lo", "core")
bf16 = jnp.bfloat16
f32 = jnp.float32
ANY = pl.BlockSpec(memory_space=pl.ANY)
SMEM = pl.BlockSpec(memory_space=pltpu.SMEM)


def fetch(value, axis, count, distance):
    return lax.ppermute(value, axis, [((i + distance) % count, i) for i in range(count)])


def toward(value, axis, sign):
    pairs = []
    for i in range(4):
        for core in range(2):
            step = sign if core == 0 else -sign
            pairs.append((((i + step) % 4) * 2 + core, i * 2 + core))
    return lax.ppermute(value, (axis, "core"), pairs)


def ring(value, axis, later=()):
    near = toward(value, axis, 1)
    value, near, later = lax.optimization_barrier((value, near, later))
    pieces = [value, near, toward(value, axis, -1), toward(near, axis, 1)]
    return pieces if isinstance(later, tuple) else (pieces, later)


def placed(pieces, position, dim):
    shape = [1] * (pieces[0].ndim + 1)
    shape[dim] = 4
    slot = jnp.arange(4).reshape(shape)
    whole = jnp.expand_dims(pieces[0], dim)
    for piece, distance in zip(pieces[1:], distances(lax.axis_index("core"))[1:]):
        whole = jnp.where(slot == (position + distance) % 4, jnp.expand_dims(piece, dim), whole)
    return whole


def distances(core):
    near = 1 + 2 * core
    return (0, near, 4 - near, 2)


def both_cores(pieces):
    return list(pieces) + [fetch(piece, "core", 2, 1) for piece in pieces]


def along_z(w_in, w_out):
    rows, width = w_in.shape[0], w_in.shape[1] // 2
    narrow = w_out.shape[1] // 2
    halves = [
        jnp.concatenate(
            [
                w_in[:, c * width : (c + 1) * width],
                w_out[:rows, c * narrow : (c + 1) * narrow],
                w_out[rows:, c * narrow : (c + 1) * narrow],
            ],
            axis=1,
        )
        for c in range(2)
    ]
    low_core, low_z = lax.axis_index("core") == 0, lax.axis_index("z_lo") == 0
    keep = jnp.where(low_core, halves[0], halves[1])
    got = fetch(jnp.where(low_core, halves[1], halves[0]), "core", 2, 1)
    pair = jnp.where(low_core, jnp.stack([keep, got]), jnp.stack([got, keep]))
    got = fetch(pair, "z_lo", 2, 1)
    quad = jnp.where(low_z, jnp.concatenate([pair, got]), jnp.concatenate([got, pair]))
    got = placed(ring(quad, "z_hi"), lax.axis_index("z_hi"), 0).reshape(16, rows, -1)
    near_in = got[:, :, :width].reshape(4, 4 * rows, width)
    near_out = jnp.concatenate(
        [got[:, :, width : width + narrow], got[:, :, width + narrow :]], axis=1
    ).reshape(4, 8 * rows, narrow)
    return near_in, near_out


def gather_weights(w_in, w_out, later):
    near_in, near_out = along_z(w_in, w_out)
    middle_in = placed(ring(near_in, "y"), lax.axis_index("y"), 1)
    middle_in = middle_in.reshape(4, -1, near_in.shape[2])
    middle_out = placed(ring(near_out, "x"), lax.axis_index("x"), 1)
    pieces_in, later = ring(middle_in, "x", later)
    pieces_out = ring(middle_out, "y")
    return both_cores(pieces_in), both_cores(pieces_out), later


def copies_in(idx, pieces, held, sems):
    x = idx[1]
    for core in range(2):
        far = distances((idx[4] + core) % 2)
        for distance, piece in zip(far, pieces[core * 4 : core * 4 + 4]):
            rows = piece.shape[1]
            for i in range(piece.shape[0]):
                at = (i * 4 + (x + distance) % 4) * rows
                pltpu.make_async_copy(
                    piece.at[i],
                    held.at[core, pl.ds(pl.multiple_of(at, rows), rows), :],
                    sems.at[core],
                ).start()


def copies_out(idx, pieces, held, sems):
    y = idx[2]
    for core in range(2):
        far = distances((idx[4] + core) % 2)
        for distance, piece in zip(far, pieces[core * 4 : core * 4 + 4]):
            pltpu.make_async_copy(
                piece, held.at[core, :, :, (y + distance) % 4], sems.at[core]
            ).start()


def arrive(held, sems, core):
    pltpu.make_async_copy(held.at[core], held.at[core], sems.at[core]).wait()


def region_of(pixel):
    return ((pixel >> 7) << 3) + ((pixel & 31) >> 2)


def split2(value):
    high = value.astype(bf16)
    return high, (value - high.astype(f32)).astype(bf16)


def split3(value):
    high = value.astype(bf16)
    rest = value - high.astype(f32)
    mid = rest.astype(bf16)
    return high, mid, (rest - mid.astype(f32)).astype(bf16)


def pool_matrix(tokens, pixels):
    token = lax.broadcasted_iota(jnp.int32, (tokens, pixels), 0)
    pixel = lax.broadcasted_iota(jnp.int32, (tokens, pixels), 1)
    return jnp.where(region_of(pixel) == token, 1.0 / 16.0, 0.0).astype(bf16)


def dot(a, b):
    return jnp.dot(a, b, preferred_element_type=f32)


def dot_t(a, b):
    return lax.dot_general(a, b, (((1,), (1,)), ((), ())), preferred_element_type=f32)


def first_kernel(idx, normed, *refs):
    pieces, (slope, pooled, held, sems) = refs[:8], refs[8:]
    copies_in(idx, pieces, held, sems)
    pixels = normed.shape[0]
    tokens = pooled.shape[1] // 2
    steps = held.shape[2] // 512

    @pl.loop(0, 2)
    def _(core):
        arrive(held, sems, core)
        at = (idx[4] + core) % 2

        @pl.loop(0, steps)
        def _(step):
            lanes = pl.ds(pl.multiple_of(step * 512, 512), 512)
            pre = dot(normed[...], held[core, :, lanes])
            cdf = 0.5 * (1.0 + lax.erf(pre * 0.7071067811865476))
            density = jnp.exp(-0.5 * pre * pre) * 0.3989422804014327
            hidden = (pre * cdf).astype(bf16)
            slope[at, :, lanes] = cdf + pre * density
            high, low = split2(dot(pool_matrix(tokens, pixels), hidden))
            pooled[at, :tokens, lanes] = high
            pooled[at, tokens:, lanes] = low


def second_kernel(idx, hidden, feats, scale, *refs):
    pieces, (unit, norm, token, held, mixed, sems) = refs[:8], refs[8:]
    copies_out(idx, pieces, held, sems)
    tokens = unit.shape[0]
    base = dot(pool_matrix(tokens, feats.shape[0]), feats[...])
    half, width = hidden.shape[2], held.shape[5]
    @pl.loop(0, 2)
    def _(core):
        arrive(held, sems, core)
        at = (idx[4] + core) % 2
        low = held[core, :2].reshape(half, width)
        high = held[core, 2:].reshape(half, width)
        both = dot(hidden[0], low) + dot(hidden[1], high)
        mixed[at] = both[:tokens] + both[tokens:]

    full = jnp.concatenate([mixed[0], mixed[1]], axis=1)
    pool = base + scale[...] * full
    inv = lax.rsqrt(jnp.sum(pool * pool, axis=1, keepdims=True) + eps_norm)
    unit[...] = pool * inv
    norm[...] = jnp.broadcast_to(inv, norm.shape)
    token[...] = (pool * inv).astype(bf16)


def third_kernel(
    idx, keys, chosen, ids, unit, norm, scale, gain, spread, slope_hbm, rows_hbm, *refs
):
    out_pieces, in_pieces = refs[:8], refs[8:16]
    (grad_conv, scaled, loss, held_out, held_in, slope, rows, mix, hid, total_ref) = refs[16:26]
    sem_out, sem_in, sem = refs[26:]
    copies_out(idx, out_pieces, held_out, sem_out)
    copies_in(idx, in_pieces, held_in, sem_in)
    copy_slope = pltpu.make_async_copy(slope_hbm, slope, sem.at[0])
    copy_slope.start()
    copy_rows = pltpu.make_async_copy(rows_hbm, rows, sem.at[1])
    copy_rows.start()
    token_grads, losses = [], []
    for r in range(keys.shape[0]):
        key = keys[r]
        count = key.shape[0]
        similar = dot_t(key, key)
        hits, logits = [], []
        for n in range(NEG + 1):
            hit = chosen[r, :, n : n + 1] == ids[...]
            hits.append(hit)
            logits.append(
                inv_temp * jnp.sum(jnp.where(hit, similar, 0.0), axis=1, keepdims=True)
            )
        exps = [jnp.exp(value) for value in logits]
        total = exps[0]
        for value in exps[1:]:
            total = total + value
        weight = jnp.zeros((count, count), f32)
        for n in range(NEG + 1):
            coef = loss_scale * inv_temp * (exps[n] / total - (1.0 if n == 0 else 0.0))
            weight = weight + jnp.where(hits[n], coef, 0.0)
        own = weight[:8] + jnp.transpose(weight)[:8]
        high, mid, low = split3(own)
        token_grads.append(dot(high, key) + dot(mid, key) + dot(low, key))
        losses.append((jnp.log(total) - logits[0])[:8])
    loss[...] = jnp.broadcast_to(
        jnp.sum(losses[0] + losses[1], axis=0, keepdims=True), loss.shape
    )
    grad_tok = jnp.concatenate(token_grads, axis=0)
    unit_v = unit[...]
    grad_pool = (grad_tok - unit_v * jnp.sum(unit_v * grad_tok, axis=1, keepdims=True)) * norm[
        :, :1
    ]
    spread_grad = grad_pool / 16.0
    scaled[...] = spread_grad
    grad_mix = (scale[...] * spread_grad).astype(bf16)
    width = held_out.shape[5]
    mix[0] = grad_mix[:, :width]
    mix[1] = grad_mix[:, width:]
    for core in range(2):
        arrive(held_out, sem_out, core)
    half = held_in.shape[2]
    tokens = grad_mix.shape[0]
    quarter = half // 2

    @pl.loop(0, 4)
    def _(z):
        part = jnp.zeros((quarter, tokens), f32)
        for core in range(2):
            at = (idx[4] + core) % 2
            part = part + dot_t(held_out[core, z].reshape(quarter, width), mix[at])
        lanes = pl.ds(pl.multiple_of((z & 1) * quarter, 128), quarter)
        for i, piece in enumerate(split3(jnp.transpose(part))):
            hid[z >> 1, i * tokens : (i + 1) * tokens, lanes] = piece

    copy_slope.wait()
    pixels = rows.shape[0]
    total_ref[...] = jnp.zeros(total_ref.shape, f32)
    @pl.loop(0, 2)
    def _(core):
        arrive(held_in, sem_in, core)
        at = (idx[4] + core) % 2

        @pl.loop(0, half // 512)
        def _(step):
            lanes = pl.ds(pl.multiple_of(step * 512, 512), 512)
            pixel = lax.broadcasted_iota(jnp.int32, (pixels, 3 * tokens), 0)
            token = lax.broadcasted_iota(jnp.int32, (pixels, 3 * tokens), 1) & (tokens - 1)
            expand = jnp.where(region_of(pixel) == token, 1.0, 0.0).astype(bf16)
            wide = dot(expand, hid[at, :, lanes])
            grad_pre = (wide * slope[at, :, lanes]).astype(bf16)
            total_ref[...] += dot_t(grad_pre, held_in[core, :, lanes])

    copy_rows.wait()
    grad_unit = total_ref[...] * gain[...]
    unit_rows = rows[...]
    mean_one = jnp.mean(grad_unit, axis=1, keepdims=True)
    mean_two = jnp.mean(grad_unit * unit_rows, axis=1, keepdims=True)
    grad_conv[...] = ((grad_unit - mean_one - unit_rows * mean_two) / spread[:, :1]).astype(bf16)


def padded_rows(cells, width):
    count = lax.axis_size(ROWS)
    ends = count - 1
    head = cells[:, :width]
    tail = cells[:, cells.shape[1] - width :]
    return jnp.concatenate(
        [
            lax.ppermute(tail, ROWS, [(i, i + 1) for i in range(ends)]),
            cells,
            lax.ppermute(head, ROWS, [(i + 1, i) for i in range(ends)]),
        ],
        axis=1,
    )


def shift_in(band, wide, moved, here):
    rows, cols, _ = band.shape
    edge = jnp.zeros((8, 128), f32)

    @pl.loop(0, rows)
    def _(i):
        wide[:8, :] = edge
        wide[8 + cols :, :] = edge
        wide[8 : 8 + cols, :] = band[i, :, here].astype(f32)
        for b in range(7):
            moved[b, i] = wide[b + 5 : b + 5 + cols, :]


def lanes_of(k):
    return pl.ds(pl.multiple_of(k * 128, 128), 128)


def tile_sums(moved, wide_taps, at, height):
    sums = [jnp.zeros((8, 128), f32) for _ in range(height)]
    for b in range(7):
        tap = [wide_taps[a * 7 + b] for a in range(7)]
        for i in range(height + 6):
            window = moved[b, i, at]
            for a in range(7):
                if 0 <= i - a < height:
                    sums[i - a] = sums[i - a] + window * tap[a]
    return sums


def widen_taps(taps, wide_taps, here):
    for i in range(49):
        wide_taps[i] = jnp.broadcast_to(taps[i : i + 1, here].astype(f32), (8, 128))


def conv_kernel(band, taps, out, wide, moved, wide_taps):
    height, cols, lanes = out.shape

    @pl.loop(0, lanes // 128)
    def _(k):
        here = lanes_of(k)
        shift_in(band, wide, moved, here)
        widen_taps(taps, wide_taps, here)

        @pl.loop(0, cols // 8)
        def _(t):
            at = pl.ds(pl.multiple_of(t * 8, 8), 8)
            for r, value in enumerate(tile_sums(moved, wide_taps, at, height)):
                out[r, at, here] = value


def back_kernel(band, taps, scaled, out, wide, moved, wide_taps, grad, grad_rows):
    height, cols, lanes = out.shape
    upper = lax.broadcasted_iota(jnp.int32, (8, 128), 0) < REGION

    @pl.loop(0, lanes // 128)
    def _(k):
        here = lanes_of(k)
        shift_in(band, wide, moved, here)
        widen_taps(taps, wide_taps, here)
        for g in range(height // REGION):
            for t in range(cols // 8):
                at = g * (cols // REGION) + 2 * t
                grad[g, t * 8 : t * 8 + 8] = jnp.where(
                    upper, scaled[at : at + 1, here], scaled[at + 1 : at + 2, here]
                )

        @pl.loop(0, cols // 8)
        def _(t):
            at = pl.ds(pl.multiple_of(t * 8, 8), 8)
            for r, value in enumerate(tile_sums(moved, wide_taps, at, height)):
                grad_rows[r, at] = grad[r // REGION, at] + value

        out[:, :, here] = grad_rows[...].astype(bf16)


def terms_kernel(band, grad_b, loss, out, wide, moved, grad):
    height, cols, lanes = grad.shape
    out[48:, :] = jnp.broadcast_to(loss[:, :1], (out.shape[0] - 48, lanes))
    for r in range(height):
        grad[r] = grad_b[r].astype(f32)

    @pl.loop(0, lanes // 128)
    def _(k):
        here = lanes_of(k)
        shift_in(band, wide, moved, here)
        for b in range(7):

            def step(t, sums):
                sums = list(sums)
                at = pl.ds(pl.multiple_of(t * 8, 8), 8)
                g = [grad[r, at, here] for r in range(height)]
                for i in range(height + 6):
                    window = moved[b, i, at]
                    for a in range(7):
                        if 0 <= i - a < height:
                            sums[a] = sums[a] + window * g[i - a]
                return tuple(sums)

            sums = lax.fori_loop(0, cols // 8, step, (jnp.zeros((8, 128), f32),) * 7)
            for a in range(7):
                out[a * 7 + b : a * 7 + b + 1, here] = jnp.sum(sums[a], axis=0, keepdims=True)


def conv_scratch(rows, cols):
    return [pltpu.VMEM((cols + 16, 128), f32), pltpu.VMEM((7, rows, cols, 128), f32)]


def conv_forward(band, taps):
    rows, cols, channels = band.shape
    lanes = channels // 4
    return pl.pallas_call(
        conv_kernel,
        grid=(4,),
        in_specs=[
            pl.BlockSpec((rows, cols, lanes), lambda i: (0, 0, i)),
            pl.BlockSpec((49, lanes), lambda i: (0, i)),
        ],
        out_specs=pl.BlockSpec((rows - 6, cols, lanes), lambda i: (0, 0, i)),
        out_shape=jax.ShapeDtypeStruct((rows - 6, cols, channels), f32),
        scratch_shapes=conv_scratch(rows, cols) + [pltpu.VMEM((49, 8, 128), f32)],
        name="depthwise",
    )(band, taps)


def conv_backward(band, taps, scaled, k, parts):
    rows, cols, channels = band.shape
    lanes = channels // parts
    return pl.pallas_call(
        back_kernel,
        grid=(1,),
        in_specs=[
            pl.BlockSpec((rows, cols, lanes), lambda i: (0, 0, k)),
            pl.BlockSpec((49, lanes), lambda i: (0, k)),
            pl.BlockSpec((scaled.shape[0], lanes), lambda i: (0, k)),
        ],
        out_specs=pl.BlockSpec((rows - 6, cols, lanes), lambda i: (0, 0, 0)),
        out_shape=jax.ShapeDtypeStruct((rows - 6, cols, lanes), bf16),
        scratch_shapes=conv_scratch(rows, cols)
        + [
            pltpu.VMEM((49, 8, 128), f32),
            pltpu.VMEM(((rows - 6) // REGION, cols, 128), f32),
            pltpu.VMEM((rows - 6, cols, 128), f32),
        ],
        name="depthwise_back",
    )(band, taps, scaled)


def kernel_terms(band, grad_conv, loss):
    height, cols, channels = grad_conv.shape
    lanes = channels // 4
    return pl.pallas_call(
        terms_kernel,
        grid=(4,),
        in_specs=[
            pl.BlockSpec((height + 6, cols, lanes), lambda i: (0, 0, i)),
            pl.BlockSpec((height, cols, lanes), lambda i: (0, 0, i)),
            pl.BlockSpec((1, 128), lambda i: (0, 0)),
        ],
        out_specs=pl.BlockSpec((64, lanes), lambda i: (0, i)),
        out_shape=jax.ShapeDtypeStruct((64, channels), f32),
        scratch_shapes=conv_scratch(height + 6, cols) + [pltpu.VMEM((height, cols, lanes), f32)],
        name="kernel_terms",
    )(band, grad_conv, loss)


def gather_tokens(message):
    near = [message] + [fetch(message, "z_hi", 4, d) for d in (1, 2, 3)]
    near = jnp.concatenate(near, axis=1)
    ahead = fetch(near, "x", 4, 1)
    behind = fetch(near, "x", 4, 3)
    far = fetch(near, "x", 4, 2)
    return jnp.concatenate([near, ahead, far, behind], axis=1)


def spread_over(value, axes):
    count = lax.axis_size(axes)
    return lax.all_to_all(jnp.broadcast_to(value[None], (count,) + value.shape), axes, 0, 0)


def own_first(own, other):
    first = lax.axis_index("core") == 0
    return jnp.where(
        first, jnp.concatenate([own, other], axis=1), jnp.concatenate([other, own], axis=1)
    )


def total_over_all(values, work):
    width = values.shape[1] // 2
    first = lax.axis_index("core") == 0
    left, right = values[:, :width], values[:, width:]
    part = jnp.where(first, left, right) + fetch(jnp.where(first, right, left), "core", 2, 1)
    part = lax.all_to_all(part.reshape(16, -1, width), ("x", "y"), 0, 0)
    done = [work[0]()]
    part, done[0] = lax.optimization_barrier((part, done[0]))
    part = spread_over(jnp.sum(part, axis=0), ("z_hi", "z_lo"))
    done.append(work[1]())
    part, done[1] = lax.optimization_barrier((part, done[1]))
    part = spread_over(jnp.sum(part, axis=0), ("x", "y"))
    done.append(work[2]())
    part, done[2] = lax.optimization_barrier((part, done[2]))
    part = part.reshape(-1, width)
    return own_first(part, fetch(part, "core", 2, 1)), done


def params(name, megabytes):
    return dict(
        name=name, compiler_params=pltpu.CompilerParams(vmem_limit_bytes=megabytes << 20)
    )


def body(features, kernel, ln_gain, layer_scale, w_in, w_out, pairs, negatives):
    height, breadth, channels = (features.shape[1], features.shape[2], features.shape[3])
    pixels = height * breadth
    reg_rows, reg_cols = (height // REGION, breadth // REGION)
    tokens = reg_rows * reg_cols
    hidden_width = w_in.shape[1]
    z, x, y, core = (lax.axis_index(name) for name in ("z_hi", "x", "y", "core"))
    idx = jnp.stack([z, x, y, lax.axis_index("z_lo"), core]).astype(jnp.int32)

    rimmed = padded_rows(features, 3)
    in_pieces, out_pieces, rimmed = gather_weights(w_in, w_out, rimmed)
    taps = kernel.reshape(49, channels)
    conv_rows = conv_forward(rimmed[0], taps).reshape(-1, channels)
    centred = conv_rows - jnp.mean(conv_rows, axis=-1, keepdims=True)
    spread = jnp.sqrt(jnp.mean(centred * centred, axis=-1, keepdims=True) + eps_layer)
    unit_rows = centred / spread
    normed = (unit_rows * ln_gain).astype(bf16)

    half = hidden_width // 2
    slope, pooled_hidden = pl.pallas_call(
        first_kernel,
        out_shape=(
            jax.ShapeDtypeStruct((2, pixels, half), f32),
            jax.ShapeDtypeStruct((2, 2 * tokens, half), bf16),
        ),
        in_specs=[SMEM, pl.BlockSpec()] + [ANY] * 8,
        scratch_shapes=[
            pltpu.VMEM((2, channels, half), bf16),
            pltpu.SemaphoreType.DMA((2,)),
        ],
        **params("expand_rows", 48),
    )(idx, normed, *in_pieces)

    width = channels // 2
    unit_tok, inv_norm, tokens_b = pl.pallas_call(
        second_kernel,
        out_shape=(
            jax.ShapeDtypeStruct((tokens, channels), f32),
            jax.ShapeDtypeStruct((tokens, 128), f32),
            jax.ShapeDtypeStruct((tokens, channels), bf16),
        ),
        in_specs=[SMEM] + [pl.BlockSpec()] * 3 + [ANY] * 8,
        scratch_shapes=[
            pltpu.VMEM((2, 4, 4, 4, hidden_width // 64, width), bf16),
            pltpu.VMEM((2, tokens, width), f32),
            pltpu.SemaphoreType.DMA((2,)),
        ],
        **params("pool_tokens", 32),
    )(
        idx,
        pooled_hidden,
        features.reshape(pixels, channels),
        layer_scale.reshape(1, channels),
        *out_pieces,
    )

    message = jnp.concatenate(
        [
            tokens_b.reshape(reg_rows, reg_cols, channels),
            jnp.pad(negatives[0].astype(bf16), ((0, 0), (0, 0), (0, 128 - NEG))),
        ],
        axis=2,
    )
    gathered = gather_tokens(message)
    keys = gathered[:, :, :channels]
    slot = jnp.arange(16, dtype=jnp.int32)
    image = ((z + slot % 4) % 4) * 4 + (x + slot // 4) % 4
    columns = jnp.arange(reg_cols, dtype=jnp.int32)
    ids = (image[:, None] * reg_cols + columns[None, :]).reshape(1, -1)
    positive = (pairs[image][:, None] * reg_cols + columns[None, :]).reshape(1, -1, 1)
    chosen = jnp.concatenate(
        [
            jnp.broadcast_to(positive, (reg_rows, positive.shape[1], 1)),
            gathered[:, :, channels : channels + NEG].astype(jnp.int32),
        ],
        axis=2,
    )

    grad_conv, scaled, loss_part = pl.pallas_call(
        third_kernel,
        out_shape=(
            jax.ShapeDtypeStruct((pixels, channels), bf16),
            jax.ShapeDtypeStruct((tokens, channels), f32),
            jax.ShapeDtypeStruct((1, 128), f32),
        ),
        in_specs=[SMEM] + [pl.BlockSpec()] * 8 + [ANY] * 18,
        scratch_shapes=[
            pltpu.VMEM((2, 4, 4, 4, hidden_width // 64, width), bf16),
            pltpu.VMEM((2, channels, half), bf16),
            pltpu.VMEM((2, pixels, half), f32),
            pltpu.VMEM((pixels, channels), f32),
            pltpu.VMEM((2, tokens, width), bf16),
            pltpu.VMEM((2, 3 * tokens, half), bf16),
            pltpu.VMEM((pixels, channels), f32),
            pltpu.SemaphoreType.DMA((2,)),
            pltpu.SemaphoreType.DMA((2,)),
            pltpu.SemaphoreType.DMA((2,)),
        ],
        **params("loss_and_back", 58),
    )(
        idx,
        keys,
        chosen,
        ids,
        unit_tok,
        inv_norm,
        layer_scale.reshape(1, channels),
        ln_gain.reshape(1, channels),
        jnp.broadcast_to(spread, (pixels, 128)),
        slope,
        unit_rows,
        *out_pieces,
        *in_pieces,
    )

    grad_conv = grad_conv.reshape(1, height, breadth, channels)
    local = kernel_terms(rimmed[0], grad_conv[0], loss_part)
    grad_rim, local = lax.optimization_barrier((padded_rows(grad_conv, 3), local))
    flipped = kernel[::-1, ::-1].reshape(49, channels)

    def back(k):
        return conv_backward(grad_rim[0], flipped, scaled, k, 3)

    summed, backs = total_over_all(local, [lambda k=k: back(k) for k in range(3)])
    grad_features = jnp.concatenate(backs, axis=2)[None]

    grad_kernel = summed[:49].reshape(7, 7, channels)
    token_count = lax.axis_size(AXES) * tokens
    loss = summed[49, 0] / float(token_count)
    return (grad_features, grad_kernel, loss)


def solution(mesh):
    split = Mesh(mesh.devices.reshape(4, 4, 4, 2, 2), AXES)
    return jax.shard_map(
        body,
        mesh=split,
        in_specs=(
            P(DP, ROWS, None, None),
            P(),
            P(),
            P(),
            P(AXES, None),
            P(AXES, None),
            P(),
            P(DP, ROWS, None, None),
        ),
        out_specs=(P(DP, ROWS, None, None), P(), P()),
        check_vma=False,
    )
```

```python
import jax
import jax.numpy as jnp
from jax import lax
from jax.experimental import pallas as pl
from jax.experimental.pallas import tpu as pltpu
from jax.sharding import Mesh, PartitionSpec as P

REGION = 4
NEG = 8
loss_scale = 1024.0
inv_temp = 16.0
eps_layer = 1e-06
eps_norm = 1e-06

AXES = ("z_hi", "x", "y", "z_lo", "core")
DP = ("z_hi", "x")
ROWS = ("y", "z_lo", "core")
bf16 = jnp.bfloat16
f32 = jnp.float32
ANY = pl.BlockSpec(memory_space=pl.ANY)
SMEM = pl.BlockSpec(memory_space=pltpu.SMEM)


def fetch(value, axis, count, distance):
    return lax.ppermute(value, axis, [((i + distance) % count, i) for i in range(count)])


def toward(value, axis, sign):
    pairs = []
    for i in range(4):
        for core in range(2):
            step = sign if core == 0 else -sign
            pairs.append((((i + step) % 4) * 2 + core, i * 2 + core))
    return lax.ppermute(value, (axis, "core"), pairs)


def ring(value, axis, later=()):
    near = toward(value, axis, 1)
    value, near, later = lax.optimization_barrier((value, near, later))
    pieces = [value, near, toward(value, axis, -1), toward(near, axis, 1)]
    return pieces if isinstance(later, tuple) else (pieces, later)


def placed(pieces, position, dim):
    shape = [1] * (pieces[0].ndim + 1)
    shape[dim] = 4
    slot = jnp.arange(4).reshape(shape)
    whole = jnp.expand_dims(pieces[0], dim)
    for piece, distance in zip(pieces[1:], distances(lax.axis_index("core"))[1:]):
        whole = jnp.where(slot == (position + distance) % 4, jnp.expand_dims(piece, dim), whole)
    return whole


def distances(core):
    near = 1 + 2 * core
    return (0, near, 4 - near, 2)


def both_cores(pieces):
    return list(pieces) + [fetch(piece, "core", 2, 1) for piece in pieces]


def along_z(w_in, w_out, features):
    rows, width = w_in.shape[0], w_in.shape[1] // 2
    narrow = w_out.shape[1] // 2
    halves = [
        jnp.concatenate(
            [
                w_in[:, c * width : (c + 1) * width],
                w_out[:rows, c * narrow : (c + 1) * narrow],
                w_out[rows:, c * narrow : (c + 1) * narrow],
            ],
            axis=1,
        )
        for c in range(2)
    ]
    low_core, low_z = lax.axis_index("core") == 0, lax.axis_index("z_lo") == 0
    keep = jnp.where(low_core, halves[0], halves[1])
    got = fetch(jnp.where(low_core, halves[1], halves[0]), "core", 2, 1)
    pair = jnp.where(low_core, jnp.stack([keep, got]), jnp.stack([got, keep]))
    got = fetch(pair, "z_lo", 2, 1)
    quad = jnp.where(low_z, jnp.concatenate([pair, got]), jnp.concatenate([got, pair]))
    features, quad = lax.optimization_barrier((features, quad))
    rimmed = padded_rows(features, 3)
    got = placed(ring(quad, "z_hi"), lax.axis_index("z_hi"), 0).reshape(16, rows, -1)
    near_in = got[:, :, :width].reshape(4, 4 * rows, width)
    near_out = jnp.concatenate(
        [got[:, :, width : width + narrow], got[:, :, width + narrow :]], axis=1
    ).reshape(4, 8 * rows, narrow)
    return lax.optimization_barrier((near_in, near_out, rimmed))


def gather_weights(w_in, w_out, features):
    near_in, near_out, rimmed = along_z(w_in, w_out, features)
    middle_in = placed(ring(near_in, "y"), lax.axis_index("y"), 1)
    middle_in = middle_in.reshape(4, -1, near_in.shape[2])
    middle_out = placed(ring(near_out, "x"), lax.axis_index("x"), 1)
    pieces_in, rimmed = ring(middle_in, "x", rimmed)
    pieces_out = ring(middle_out, "y")
    return both_cores(pieces_in), both_cores(pieces_out), rimmed


def copies_in(idx, pieces, held, sems):
    x = idx[1]
    for core in range(2):
        far = distances((idx[4] + core) % 2)
        for distance, piece in zip(far, pieces[core * 4 : core * 4 + 4]):
            rows = piece.shape[1]
            for i in range(piece.shape[0]):
                at = (i * 4 + (x + distance) % 4) * rows
                pltpu.make_async_copy(
                    piece.at[i],
                    held.at[core, pl.ds(pl.multiple_of(at, rows), rows), :],
                    sems.at[core],
                ).start()


def copies_out(idx, pieces, held, sems):
    y = idx[2]
    for core in range(2):
        far = distances((idx[4] + core) % 2)
        for distance, piece in zip(far, pieces[core * 4 : core * 4 + 4]):
            pltpu.make_async_copy(
                piece, held.at[core, :, :, (y + distance) % 4], sems.at[core]
            ).start()


def arrive(held, sems, core):
    pltpu.make_async_copy(held.at[core], held.at[core], sems.at[core]).wait()


def region_of(pixel):
    return ((pixel >> 7) << 3) + ((pixel & 31) >> 2)


def split2(value):
    high = value.astype(bf16)
    return high, (value - high.astype(f32)).astype(bf16)


def split3(value):
    high = value.astype(bf16)
    rest = value - high.astype(f32)
    mid = rest.astype(bf16)
    return high, mid, (rest - mid.astype(f32)).astype(bf16)


def pool_matrix(tokens, pixels):
    token = lax.broadcasted_iota(jnp.int32, (tokens, pixels), 0)
    pixel = lax.broadcasted_iota(jnp.int32, (tokens, pixels), 1)
    return jnp.where(region_of(pixel) == token, 1.0 / 16.0, 0.0).astype(bf16)


def dot(a, b):
    return jnp.dot(a, b, preferred_element_type=f32)


def dot_t(a, b):
    return lax.dot_general(a, b, (((1,), (1,)), ((), ())), preferred_element_type=f32)


def first_kernel(idx, normed, *refs):
    pieces, (slope, pooled, held, sems) = refs[:8], refs[8:]
    copies_in(idx, pieces, held, sems)
    pixels = normed.shape[0]
    tokens = pooled.shape[1] // 2
    steps = held.shape[2] // 512

    @pl.loop(0, 2)
    def _(core):
        arrive(held, sems, core)
        at = (idx[4] + core) % 2

        @pl.loop(0, steps)
        def _(step):
            lanes = pl.ds(pl.multiple_of(step * 512, 512), 512)
            pre = dot(normed[...], held[core, :, lanes])
            cdf = 0.5 * (1.0 + lax.erf(pre * 0.7071067811865476))
            density = jnp.exp(-0.5 * pre * pre) * 0.3989422804014327
            hidden = (pre * cdf).astype(bf16)
            slope[at, :, lanes] = cdf + pre * density
            high, low = split2(dot(pool_matrix(tokens, pixels), hidden))
            pooled[at, :tokens, lanes] = high
            pooled[at, tokens:, lanes] = low


def second_kernel(idx, hidden, feats, scale, *refs):
    pieces, (unit, norm, token, held, mixed, sems) = refs[:8], refs[8:]
    copies_out(idx, pieces, held, sems)
    tokens = unit.shape[0]
    base = dot(pool_matrix(tokens, feats.shape[0]), feats[...])
    half, width = hidden.shape[2], held.shape[5]
    @pl.loop(0, 2)
    def _(core):
        arrive(held, sems, core)
        at = (idx[4] + core) % 2
        low = held[core, :2].reshape(half, width)
        high = held[core, 2:].reshape(half, width)
        both = dot(hidden[0], low) + dot(hidden[1], high)
        mixed[at] = both[:tokens] + both[tokens:]

    full = jnp.concatenate([mixed[0], mixed[1]], axis=1)
    pool = base + scale[...] * full
    inv = lax.rsqrt(jnp.sum(pool * pool, axis=1, keepdims=True) + eps_norm)
    unit[...] = pool * inv
    norm[...] = jnp.broadcast_to(inv, norm.shape)
    token[...] = (pool * inv).astype(bf16)


def third_kernel(
    idx, keys, positive, ids, unit, norm, scale, gain, spread, slope_hbm, rows_hbm, *refs
):
    out_pieces, in_pieces = refs[:8], refs[8:16]
    (grad_conv, scaled, loss, held_out, held_in, slope, rows, mix, hid, total_ref) = refs[16:26]
    sem_out, sem_in, sem = refs[26:]
    copies_out(idx, out_pieces, held_out, sem_out)
    copies_in(idx, in_pieces, held_in, sem_in)
    copy_slope = pltpu.make_async_copy(slope_hbm, slope, sem.at[0])
    copy_slope.start()
    copy_rows = pltpu.make_async_copy(rows_hbm, rows, sem.at[1])
    copy_rows.start()
    token_grads, losses = [], []
    channels = unit.shape[1]
    for r in range(keys.shape[0]):
        key = keys[r, :, :channels]
        others = keys[r, :, channels:].astype(f32)
        count = key.shape[0]
        similar = dot_t(key, key)
        hits, logits = [], []
        for n in range(NEG + 1):
            hit = (positive[:, :1] if n == 0 else others[:, n - 1 : n]) == ids[...]
            hits.append(hit)
            logits.append(
                inv_temp * jnp.sum(jnp.where(hit, similar, 0.0), axis=1, keepdims=True)
            )
        exps = [jnp.exp(value) for value in logits]
        total = exps[0]
        for value in exps[1:]:
            total = total + value
        weight = jnp.zeros((count, count), f32)
        for n in range(NEG + 1):
            coef = loss_scale * inv_temp * (exps[n] / total - (1.0 if n == 0 else 0.0))
            weight = weight + jnp.where(hits[n], coef, 0.0)
        own = weight[:8] + jnp.transpose(weight)[:8]
        high, mid, low = split3(own)
        token_grads.append(dot(high, key) + dot(mid, key) + dot(low, key))
        losses.append((jnp.log(total) - logits[0])[:8])
    loss[...] = jnp.broadcast_to(
        jnp.sum(losses[0] + losses[1], axis=0, keepdims=True), loss.shape
    )
    grad_tok = jnp.concatenate(token_grads, axis=0)
    unit_v = unit[...]
    grad_pool = (grad_tok - unit_v * jnp.sum(unit_v * grad_tok, axis=1, keepdims=True)) * norm[
        :, :1
    ]
    spread_grad = grad_pool / 16.0
    scaled[...] = spread_grad
    grad_mix = (scale[...] * spread_grad).astype(bf16)
    width = held_out.shape[5]
    mix[0] = grad_mix[:, :width]
    mix[1] = grad_mix[:, width:]
    for core in range(2):
        arrive(held_out, sem_out, core)
    half = held_in.shape[2]
    tokens = grad_mix.shape[0]
    quarter = half // 2

    @pl.loop(0, 4)
    def _(z):
        part = jnp.zeros((quarter, tokens), f32)
        for core in range(2):
            at = (idx[4] + core) % 2
            part = part + dot_t(held_out[core, z].reshape(quarter, width), mix[at])
        lanes = pl.ds(pl.multiple_of((z & 1) * quarter, 128), quarter)
        for i, piece in enumerate(split3(jnp.transpose(part))):
            hid[z >> 1, i * tokens : (i + 1) * tokens, lanes] = piece

    copy_slope.wait()
    pixels = rows.shape[0]
    total_ref[...] = jnp.zeros(total_ref.shape, f32)
    @pl.loop(0, 2)
    def _(core):
        arrive(held_in, sem_in, core)
        at = (idx[4] + core) % 2

        @pl.loop(0, half // 512)
        def _(step):
            lanes = pl.ds(pl.multiple_of(step * 512, 512), 512)
            pixel = lax.broadcasted_iota(jnp.int32, (pixels, 3 * tokens), 0)
            token = lax.broadcasted_iota(jnp.int32, (pixels, 3 * tokens), 1) & (tokens - 1)
            expand = jnp.where(region_of(pixel) == token, 1.0, 0.0).astype(bf16)
            wide = dot(expand, hid[at, :, lanes])
            grad_pre = (wide * slope[at, :, lanes]).astype(bf16)
            total_ref[...] += dot_t(grad_pre, held_in[core, :, lanes])

    copy_rows.wait()
    grad_unit = total_ref[...] * gain[...]
    unit_rows = rows[...]
    mean_one = jnp.mean(grad_unit, axis=1, keepdims=True)
    mean_two = jnp.mean(grad_unit * unit_rows, axis=1, keepdims=True)
    grad_conv[...] = ((grad_unit - mean_one - unit_rows * mean_two) / spread[:, :1]).astype(bf16)


def padded_rows(cells, width):
    count = lax.axis_size(ROWS)
    ends = count - 1
    head = cells[:, :width]
    tail = cells[:, cells.shape[1] - width :]
    return jnp.concatenate(
        [
            lax.ppermute(tail, ROWS, [(i, i + 1) for i in range(ends)]),
            cells,
            lax.ppermute(head, ROWS, [(i + 1, i) for i in range(ends)]),
        ],
        axis=1,
    )


def shift_in(band, wide, moved, here):
    rows, cols, _ = band.shape
    edge = jnp.zeros((8, 128), f32)

    @pl.loop(0, rows)
    def _(i):
        wide[:8, :] = edge
        wide[8 + cols :, :] = edge
        wide[8 : 8 + cols, :] = band[i, :, here].astype(f32)
        for b in range(7):
            moved[b, i] = wide[b + 5 : b + 5 + cols, :]


def lanes_of(k):
    return pl.ds(pl.multiple_of(k * 128, 128), 128)


def tile_sums(moved, wide_taps, at, height):
    sums = [jnp.zeros((8, 128), f32) for _ in range(height)]
    for b in range(7):
        tap = [wide_taps[a * 7 + b] for a in range(7)]
        for i in range(height + 6):
            window = moved[b, i, at]
            for a in range(7):
                if 0 <= i - a < height:
                    sums[i - a] = sums[i - a] + window * tap[a]
    return sums


def widen_taps(taps, wide_taps, here):
    for i in range(49):
        wide_taps[i] = jnp.broadcast_to(taps[i : i + 1, here].astype(f32), (8, 128))


def conv_kernel(band, taps, out, wide, moved, wide_taps):
    height, cols, lanes = out.shape

    @pl.loop(0, lanes // 128)
    def _(k):
        here = lanes_of(k)
        shift_in(band, wide, moved, here)
        widen_taps(taps, wide_taps, here)

        @pl.loop(0, cols // 8)
        def _(t):
            at = pl.ds(pl.multiple_of(t * 8, 8), 8)
            for r, value in enumerate(tile_sums(moved, wide_taps, at, height)):
                out[r, at, here] = value


def back_kernel(band, taps, scaled, *refs):
    out, wide, moved, wide_taps, grad, grad_rows = refs[-6:]
    height, cols, lanes = out.shape
    upper = lax.broadcasted_iota(jnp.int32, (8, 128), 0) < REGION

    @pl.loop(0, lanes // 128)
    def _(k):
        here = lanes_of(k)
        shift_in(band, wide, moved, here)
        widen_taps(taps, wide_taps, here)
        for g in range(height // REGION):
            for t in range(cols // 8):
                at = g * (cols // REGION) + 2 * t
                grad[g, t * 8 : t * 8 + 8] = jnp.where(
                    upper, scaled[at : at + 1, here], scaled[at + 1 : at + 2, here]
                )

        @pl.loop(0, cols // 8)
        def _(t):
            at = pl.ds(pl.multiple_of(t * 8, 8), 8)
            for r, value in enumerate(tile_sums(moved, wide_taps, at, height)):
                grad_rows[r, at] = grad[r // REGION, at] + value

        out[:, :, here] = grad_rows[...].astype(bf16)


def terms_kernel(band, grad_b, loss, out, wide, moved, grad):
    height, cols, lanes = grad.shape
    out[48:, :] = jnp.broadcast_to(loss[:, :1], (out.shape[0] - 48, lanes))
    for r in range(height):
        grad[r] = grad_b[r].astype(f32)

    @pl.loop(0, lanes // 128)
    def _(k):
        here = lanes_of(k)
        shift_in(band, wide, moved, here)
        for b in range(7):

            def step(t, sums):
                sums = list(sums)
                at = pl.ds(pl.multiple_of(t * 8, 8), 8)
                g = [grad[r, at, here] for r in range(height)]
                for i in range(height + 6):
                    window = moved[b, i, at]
                    for a in range(7):
                        if 0 <= i - a < height:
                            sums[a] = sums[a] + window * g[i - a]
                return tuple(sums)

            sums = lax.fori_loop(0, cols // 8, step, (jnp.zeros((8, 128), f32),) * 7)
            for a in range(7):
                out[a * 7 + b : a * 7 + b + 1, here] = jnp.sum(sums[a], axis=0, keepdims=True)


def conv_scratch(rows, cols):
    return [pltpu.VMEM((cols + 16, 128), f32), pltpu.VMEM((7, rows, cols, 128), f32)]


def conv_forward(band, taps):
    rows, cols, channels = band.shape
    lanes = channels // 4
    return pl.pallas_call(
        conv_kernel,
        grid=(4,),
        in_specs=[
            pl.BlockSpec((rows, cols, lanes), lambda i: (0, 0, i)),
            pl.BlockSpec((49, lanes), lambda i: (0, i)),
        ],
        out_specs=pl.BlockSpec((rows - 6, cols, lanes), lambda i: (0, 0, i)),
        out_shape=jax.ShapeDtypeStruct((rows - 6, cols, channels), f32),
        scratch_shapes=conv_scratch(rows, cols) + [pltpu.VMEM((49, 8, 128), f32)],
        name="depthwise",
    )(band, taps)


def conv_backward(band, taps, scaled, k, parts, before):
    rows, cols, channels = band.shape
    lanes = channels // parts
    return pl.pallas_call(
        back_kernel,
        grid=(1,),
        in_specs=[
            pl.BlockSpec((rows, cols, lanes), lambda i: (0, 0, k)),
            pl.BlockSpec((49, lanes), lambda i: (0, k)),
            pl.BlockSpec((scaled.shape[0], lanes), lambda i: (0, k)),
        ]
        + [ANY] * len(before),
        out_specs=pl.BlockSpec((rows - 6, cols, lanes), lambda i: (0, 0, k)),
        out_shape=jax.ShapeDtypeStruct((rows - 6, cols, channels), bf16),
        input_output_aliases={3: 0} if before else {},
        scratch_shapes=conv_scratch(rows, cols)
        + [
            pltpu.VMEM((49, 8, 128), f32),
            pltpu.VMEM(((rows - 6) // REGION, cols, 128), f32),
            pltpu.VMEM((rows - 6, cols, 128), f32),
        ],
        name="depthwise_back",
    )(band, taps, scaled, *before)


def kernel_terms(band, grad_conv, loss):
    height, cols, channels = grad_conv.shape
    lanes = channels // 4
    return pl.pallas_call(
        terms_kernel,
        grid=(4,),
        in_specs=[
            pl.BlockSpec((height + 6, cols, lanes), lambda i: (0, 0, i)),
            pl.BlockSpec((height, cols, lanes), lambda i: (0, 0, i)),
            pl.BlockSpec((1, 128), lambda i: (0, 0)),
        ],
        out_specs=pl.BlockSpec((64, lanes), lambda i: (0, i)),
        out_shape=jax.ShapeDtypeStruct((64, channels), f32),
        scratch_shapes=conv_scratch(height + 6, cols) + [pltpu.VMEM((height, cols, lanes), f32)],
        name="kernel_terms",
    )(band, grad_conv, loss)


def gather_tokens(message):
    near = [message] + [fetch(message, "z_hi", 4, d) for d in (1, 2, 3)]
    near = jnp.concatenate(near, axis=1)
    ahead = fetch(near, "x", 4, 1)
    behind = fetch(near, "x", 4, 3)
    far = fetch(near, "x", 4, 2)
    return jnp.concatenate([near, ahead, far, behind], axis=1)


def spread_over(value, axes):
    count = lax.axis_size(axes)
    return lax.all_to_all(jnp.broadcast_to(value[None], (count,) + value.shape), axes, 0, 0)


def own_first(own, other):
    first = lax.axis_index("core") == 0
    return jnp.where(
        first, jnp.concatenate([own, other], axis=1), jnp.concatenate([other, own], axis=1)
    )


def total_over_all(values, work):
    width = values.shape[1] // 2
    first = lax.axis_index("core") == 0
    left, right = values[:, :width], values[:, width:]
    part = jnp.where(first, left, right) + fetch(jnp.where(first, right, left), "core", 2, 1)
    part = lax.all_to_all(part.reshape(16, -1, width), ("x", "y"), 0, 0)
    done = work(0)
    part, done = lax.optimization_barrier((part, done))
    part = spread_over(jnp.sum(part, axis=0), ("z_hi", "z_lo"))
    done = work(1, done)
    part, done = lax.optimization_barrier((part, done))
    part = spread_over(jnp.sum(part, axis=0), ("x", "y"))
    done = work(2, done)
    part, done = lax.optimization_barrier((part, done))
    part = part.reshape(-1, width)
    return own_first(part, fetch(part, "core", 2, 1)), done


def params(name, megabytes):
    return dict(
        name=name, compiler_params=pltpu.CompilerParams(vmem_limit_bytes=megabytes << 20)
    )


def body(features, kernel, ln_gain, layer_scale, w_in, w_out, pairs, negatives):
    height, breadth, channels = (features.shape[1], features.shape[2], features.shape[3])
    pixels = height * breadth
    reg_rows, reg_cols = (height // REGION, breadth // REGION)
    tokens = reg_rows * reg_cols
    hidden_width = w_in.shape[1]
    z, x, y, core = (lax.axis_index(name) for name in ("z_hi", "x", "y", "core"))
    idx = jnp.stack([z, x, y, lax.axis_index("z_lo"), core]).astype(jnp.int32)

    in_pieces, out_pieces, rimmed = gather_weights(w_in, w_out, features)
    taps = kernel.reshape(49, channels)
    conv_rows = conv_forward(rimmed[0], taps).reshape(-1, channels)
    centred = conv_rows - jnp.mean(conv_rows, axis=-1, keepdims=True)
    spread = jnp.sqrt(jnp.mean(centred * centred, axis=-1, keepdims=True) + eps_layer)
    unit_rows = centred / spread
    normed = (unit_rows * ln_gain).astype(bf16)
    spread = jnp.broadcast_to(spread, (pixels, 128))
    normed, spread = lax.optimization_barrier((normed, spread))

    half = hidden_width // 2
    slope, pooled_hidden = pl.pallas_call(
        first_kernel,
        out_shape=(
            jax.ShapeDtypeStruct((2, pixels, half), f32),
            jax.ShapeDtypeStruct((2, 2 * tokens, half), bf16),
        ),
        in_specs=[SMEM, pl.BlockSpec()] + [ANY] * 8,
        scratch_shapes=[
            pltpu.VMEM((2, channels, half), bf16),
            pltpu.SemaphoreType.DMA((2,)),
        ],
        **params("expand_rows", 48),
    )(idx, normed, *in_pieces)

    width = channels // 2
    unit_tok, inv_norm, tokens_b = pl.pallas_call(
        second_kernel,
        out_shape=(
            jax.ShapeDtypeStruct((tokens, channels), f32),
            jax.ShapeDtypeStruct((tokens, 128), f32),
            jax.ShapeDtypeStruct((tokens, channels), bf16),
        ),
        in_specs=[SMEM] + [pl.BlockSpec()] * 3 + [ANY] * 8,
        scratch_shapes=[
            pltpu.VMEM((2, 4, 4, 4, hidden_width // 64, width), bf16),
            pltpu.VMEM((2, tokens, width), f32),
            pltpu.SemaphoreType.DMA((2,)),
        ],
        **params("pool_tokens", 32),
    )(
        idx,
        pooled_hidden,
        features.reshape(pixels, channels),
        layer_scale.reshape(1, channels),
        *out_pieces,
    )

    message = jnp.concatenate(
        [
            tokens_b.reshape(reg_rows, reg_cols, channels),
            jnp.pad(negatives[0].astype(bf16), ((0, 0), (0, 0), (0, 128 - NEG))),
        ],
        axis=2,
    )
    gathered = gather_tokens(message)
    slot = jnp.arange(16, dtype=jnp.int32)
    image = ((z + slot % 4) % 4) * 4 + (x + slot // 4) % 4
    columns = jnp.arange(reg_cols, dtype=jnp.int32)
    ids = (image[:, None] * reg_cols + columns[None, :]).reshape(1, -1).astype(f32)
    positive = (pairs[image][:, None] * reg_cols + columns[None, :]).reshape(-1, 1)
    positive = jnp.broadcast_to(positive, (positive.shape[0], 128)).astype(f32)

    grad_conv, scaled, loss_part = pl.pallas_call(
        third_kernel,
        out_shape=(
            jax.ShapeDtypeStruct((pixels, channels), bf16),
            jax.ShapeDtypeStruct((tokens, channels), f32),
            jax.ShapeDtypeStruct((1, 128), f32),
        ),
        in_specs=[SMEM] + [pl.BlockSpec()] * 8 + [ANY] * 18,
        scratch_shapes=[
            pltpu.VMEM((2, 4, 4, 4, hidden_width // 64, width), bf16),
            pltpu.VMEM((2, channels, half), bf16),
            pltpu.VMEM((2, pixels, half), f32),
            pltpu.VMEM((pixels, channels), f32),
            pltpu.VMEM((2, tokens, width), bf16),
            pltpu.VMEM((2, 3 * tokens, half), bf16),
            pltpu.VMEM((pixels, channels), f32),
            pltpu.SemaphoreType.DMA((2,)),
            pltpu.SemaphoreType.DMA((2,)),
            pltpu.SemaphoreType.DMA((2,)),
        ],
        **params("loss_and_back", 58),
    )(
        idx,
        gathered,
        positive,
        ids,
        unit_tok,
        inv_norm,
        layer_scale.reshape(1, channels),
        ln_gain.reshape(1, channels),
        spread,
        slope,
        unit_rows,
        *out_pieces,
        *in_pieces,
    )

    grad_conv = grad_conv.reshape(1, height, breadth, channels)
    local = kernel_terms(rimmed[0], grad_conv[0], loss_part)
    grad_rim, local = lax.optimization_barrier((padded_rows(grad_conv, 3), local))
    flipped = kernel[::-1, ::-1].reshape(49, channels)

    def back(k, *before):
        return conv_backward(grad_rim[0], flipped, scaled, k, 3, before)

    summed, grad_features = total_over_all(local, back)
    grad_features = grad_features[None]

    grad_kernel = summed[:49].reshape(7, 7, channels)
    token_count = lax.axis_size(AXES) * tokens
    loss = summed[49, 0] / float(token_count)
    return (grad_features, grad_kernel, loss)


def solution(mesh):
    split = Mesh(mesh.devices.reshape(4, 4, 4, 2, 2), AXES)
    return jax.shard_map(
        body,
        mesh=split,
        in_specs=(
            P(DP, ROWS, None, None),
            P(),
            P(),
            P(),
            P(AXES, None),
            P(AXES, None),
            P(),
            P(DP, ROWS, None, None),
        ),
        out_specs=(P(DP, ROWS, None, None), P(), P()),
        check_vma=False,
    )
```

```python
import jax
import jax.numpy as jnp
from jax import lax
from jax.experimental import pallas as pl
from jax.experimental.pallas import tpu as pltpu
from jax.sharding import Mesh, PartitionSpec as P

REGION = 4
NEG = 8
loss_scale = 1024.0
inv_temp = 16.0
eps_layer = 1e-06
eps_norm = 1e-06

AXES = ("z_hi", "x", "y", "z_lo", "core")
DP = ("z_hi", "x")
ROWS = ("y", "z_lo", "core")
bf16 = jnp.bfloat16
f32 = jnp.float32
ANY = pl.BlockSpec(memory_space=pl.ANY)
SMEM = pl.BlockSpec(memory_space=pltpu.SMEM)


def fetch(value, axis, count, distance):
    return lax.ppermute(value, axis, [((i + distance) % count, i) for i in range(count)])


def toward(value, axis, sign):
    pairs = []
    for i in range(4):
        for core in range(2):
            step = sign if core == 0 else -sign
            pairs.append((((i + step) % 4) * 2 + core, i * 2 + core))
    return lax.ppermute(value, (axis, "core"), pairs)


def ring(value, axis):
    near = toward(value, axis, 1)
    value, near = lax.optimization_barrier((value, near))
    return [value, near, toward(value, axis, -1), toward(near, axis, 1)]


def placed(pieces, position, dim):
    shape = [1] * (pieces[0].ndim + 1)
    shape[dim] = 4
    slot = jnp.arange(4).reshape(shape)
    whole = jnp.expand_dims(pieces[0], dim)
    for piece, distance in zip(pieces[1:], distances(lax.axis_index("core"))[1:]):
        whole = jnp.where(slot == (position + distance) % 4, jnp.expand_dims(piece, dim), whole)
    return whole


def distances(core):
    near = 1 + 2 * core
    return (0, near, 4 - near, 2)


def both_cores(pieces):
    return list(pieces) + [fetch(piece, "core", 2, 1) for piece in pieces]


def along_z(w_in, w_out):
    rows, width = w_in.shape[0], w_in.shape[1] // 2
    narrow = w_out.shape[1] // 2
    halves = [
        jnp.concatenate(
            [
                w_in[:, c * width : (c + 1) * width],
                w_out[:rows, c * narrow : (c + 1) * narrow],
                w_out[rows:, c * narrow : (c + 1) * narrow],
            ],
            axis=1,
        )
        for c in range(2)
    ]
    low_core, low_z = lax.axis_index("core") == 0, lax.axis_index("z_lo") == 0
    keep = jnp.where(low_core, halves[0], halves[1])
    got = fetch(jnp.where(low_core, halves[1], halves[0]), "core", 2, 1)
    pair = jnp.where(low_core, jnp.stack([keep, got]), jnp.stack([got, keep]))
    got = fetch(pair, "z_lo", 2, 1)
    quad = jnp.where(low_z, jnp.concatenate([pair, got]), jnp.concatenate([got, pair]))
    got = placed(ring(quad, "z_hi"), lax.axis_index("z_hi"), 0).reshape(16, rows, -1)
    near_in = got[:, :, :width].reshape(4, 4 * rows, width)
    near_out = jnp.concatenate(
        [got[:, :, width : width + narrow], got[:, :, width + narrow :]], axis=1
    ).reshape(4, 8 * rows, narrow)
    return near_in, near_out


def gather_weights(w_in, w_out, rimmed):
    near_in, near_out = along_z(w_in, w_out)
    middle_in = placed(ring(near_in, "y"), lax.axis_index("y"), 1)
    middle_in = middle_in.reshape(4, -1, near_in.shape[2])
    middle_out = placed(ring(near_out, "x"), lax.axis_index("x"), 1)
    pieces_in = ring(middle_in, "x")
    rimmed, _ = lax.optimization_barrier((rimmed, pieces_in[1]))
    pieces_out = ring(middle_out, "y")
    return pieces_in, pieces_out, rimmed


def copies_in(idx, pieces, held, sems):
    x = idx[1]
    for core in range(2):
        far = distances((idx[4] + core) % 2)
        for distance, piece in zip(far, pieces[core * 4 : core * 4 + 4]):
            rows = piece.shape[1]
            for i in range(piece.shape[0]):
                at = (i * 4 + (x + distance) % 4) * rows
                pltpu.make_async_copy(
                    piece.at[i],
                    held.at[core, pl.ds(pl.multiple_of(at, rows), rows), :],
                    sems.at[core],
                ).start()


def copies_out(idx, pieces, held, sems):
    y = idx[2]
    for core in range(2):
        far = distances((idx[4] + core) % 2)
        for distance, piece in zip(far, pieces[core * 4 : core * 4 + 4]):
            pltpu.make_async_copy(
                piece, held.at[core, :, :, (y + distance) % 4], sems.at[core]
            ).start()


def arrive(held, sems, core):
    pltpu.make_async_copy(held.at[core], held.at[core], sems.at[core]).wait()


def region_of(pixel):
    return ((pixel >> 7) << 3) + ((pixel & 31) >> 2)


def split2(value):
    high = value.astype(bf16)
    return high, (value - high.astype(f32)).astype(bf16)


def split3(value):
    high = value.astype(bf16)
    rest = value - high.astype(f32)
    mid = rest.astype(bf16)
    return high, mid, (rest - mid.astype(f32)).astype(bf16)


def pool_matrix(tokens, pixels):
    token = lax.broadcasted_iota(jnp.int32, (tokens, pixels), 0)
    pixel = lax.broadcasted_iota(jnp.int32, (tokens, pixels), 1)
    return jnp.where(region_of(pixel) == token, 1.0 / 16.0, 0.0).astype(bf16)


def dot(a, b):
    return jnp.dot(a, b, preferred_element_type=f32)


def dot_t(a, b):
    return lax.dot_general(a, b, (((1,), (1,)), ((), ())), preferred_element_type=f32)


def first_kernel(idx, normed, *refs):
    pieces, (slope, pooled, held, sems) = refs[:8], refs[8:]
    copies_in(idx, pieces, held, sems)
    pixels = normed.shape[0]
    tokens = pooled.shape[1] // 2
    steps = held.shape[2] // 512

    @pl.loop(0, 2)
    def _(core):
        arrive(held, sems, core)
        at = (idx[4] + core) % 2

        @pl.loop(0, steps)
        def _(step):
            lanes = pl.ds(pl.multiple_of(step * 512, 512), 512)
            pre = dot(normed[...], held[core, :, lanes])
            cdf = 0.5 * (1.0 + lax.erf(pre * 0.7071067811865476))
            density = jnp.exp(-0.5 * pre * pre) * 0.3989422804014327
            hidden = (pre * cdf).astype(bf16)
            slope[at, :, lanes] = cdf + pre * density
            high, low = split2(dot(pool_matrix(tokens, pixels), hidden))
            pooled[at, :tokens, lanes] = high
            pooled[at, tokens:, lanes] = low


def second_kernel(idx, hidden, feats, scale, *refs):
    pieces, (unit, norm, token, held, mixed, sems) = refs[:8], refs[8:]
    copies_out(idx, pieces, held, sems)
    tokens = unit.shape[0]
    base = dot(pool_matrix(tokens, feats.shape[0]), feats[...])
    half, width = hidden.shape[2], held.shape[5]
    @pl.loop(0, 2)
    def _(core):
        arrive(held, sems, core)
        at = (idx[4] + core) % 2
        low = held[core, :2].reshape(half, width)
        high = held[core, 2:].reshape(half, width)
        both = dot(hidden[0], low) + dot(hidden[1], high)
        mixed[at] = both[:tokens] + both[tokens:]

    full = jnp.concatenate([mixed[0], mixed[1]], axis=1)
    pool = base + scale[...] * full
    inv = lax.rsqrt(jnp.sum(pool * pool, axis=1, keepdims=True) + eps_norm)
    unit[...] = pool * inv
    norm[...] = jnp.broadcast_to(inv, norm.shape)
    token[...] = (pool * inv).astype(bf16)


def third_kernel(
    idx, keys, positive, ids, unit, norm, scale, gain, spread, slope_hbm, rows_hbm, *refs
):
    out_pieces, in_pieces = refs[:8], refs[8:16]
    (grad_conv, scaled, loss, held_out, held_in, slope, rows, mix, hid, total_ref) = refs[16:26]
    sem_out, sem_in, sem = refs[26:]
    copies_out(idx, out_pieces, held_out, sem_out)
    copies_in(idx, in_pieces, held_in, sem_in)
    copy_slope = pltpu.make_async_copy(slope_hbm, slope, sem.at[0])
    copy_slope.start()
    copy_rows = pltpu.make_async_copy(rows_hbm, rows, sem.at[1])
    copy_rows.start()
    token_grads, losses = [], []
    channels = unit.shape[1]
    for r in range(keys.shape[0]):
        key = keys[r, :, :channels]
        others = keys[r, :, channels:].astype(f32)
        count = key.shape[0]
        similar = dot_t(key, key)
        hits, logits = [], []
        for n in range(NEG + 1):
            hit = (positive[:, :1] if n == 0 else others[:, n - 1 : n]) == ids[...]
            hits.append(hit)
            logits.append(
                inv_temp * jnp.sum(jnp.where(hit, similar, 0.0), axis=1, keepdims=True)
            )
        exps = [jnp.exp(value) for value in logits]
        total = exps[0]
        for value in exps[1:]:
            total = total + value
        weight = jnp.zeros((count, count), f32)
        for n in range(NEG + 1):
            coef = loss_scale * inv_temp * (exps[n] / total - (1.0 if n == 0 else 0.0))
            weight = weight + jnp.where(hits[n], coef, 0.0)
        own = weight[:8] + jnp.transpose(weight)[:8]
        high, mid, low = split3(own)
        token_grads.append(dot(high, key) + dot(mid, key) + dot(low, key))
        losses.append((jnp.log(total) - logits[0])[:8])
    loss[...] = jnp.broadcast_to(
        jnp.sum(losses[0] + losses[1], axis=0, keepdims=True), loss.shape
    )
    grad_tok = jnp.concatenate(token_grads, axis=0)
    unit_v = unit[...]
    grad_pool = (grad_tok - unit_v * jnp.sum(unit_v * grad_tok, axis=1, keepdims=True)) * norm[
        :, :1
    ]
    spread_grad = grad_pool / 16.0
    scaled[...] = spread_grad
    grad_mix = (scale[...] * spread_grad).astype(bf16)
    width = held_out.shape[5]
    mix[0] = grad_mix[:, :width]
    mix[1] = grad_mix[:, width:]
    for core in range(2):
        arrive(held_out, sem_out, core)
    half = held_in.shape[2]
    tokens = grad_mix.shape[0]
    quarter = half // 2

    @pl.loop(0, 4)
    def _(z):
        part = jnp.zeros((quarter, tokens), f32)
        for core in range(2):
            at = (idx[4] + core) % 2
            part = part + dot_t(held_out[core, z].reshape(quarter, width), mix[at])
        lanes = pl.ds(pl.multiple_of((z & 1) * quarter, 128), quarter)
        for i, piece in enumerate(split3(jnp.transpose(part))):
            hid[z >> 1, i * tokens : (i + 1) * tokens, lanes] = piece

    copy_slope.wait()
    pixels = rows.shape[0]
    total_ref[...] = jnp.zeros(total_ref.shape, f32)
    @pl.loop(0, 2)
    def _(core):
        arrive(held_in, sem_in, core)
        at = (idx[4] + core) % 2

        @pl.loop(0, half // 512)
        def _(step):
            lanes = pl.ds(pl.multiple_of(step * 512, 512), 512)
            pixel = lax.broadcasted_iota(jnp.int32, (pixels, 3 * tokens), 0)
            token = lax.broadcasted_iota(jnp.int32, (pixels, 3 * tokens), 1) & (tokens - 1)
            expand = jnp.where(region_of(pixel) == token, 1.0, 0.0).astype(bf16)
            wide = dot(expand, hid[at, :, lanes])
            grad_pre = (wide * slope[at, :, lanes]).astype(bf16)
            total_ref[...] += dot_t(grad_pre, held_in[core, :, lanes])

    copy_rows.wait()
    grad_unit = total_ref[...] * gain[...]
    unit_rows = rows[...]
    mean_one = jnp.mean(grad_unit, axis=1, keepdims=True)
    mean_two = jnp.mean(grad_unit * unit_rows, axis=1, keepdims=True)
    grad_conv[...] = ((grad_unit - mean_one - unit_rows * mean_two) / spread[:, :1]).astype(bf16)


def padded_rows(cells, width):
    count = lax.axis_size(ROWS)
    ends = count - 1
    head = cells[:, :width]
    tail = cells[:, cells.shape[1] - width :]
    return jnp.concatenate(
        [
            lax.ppermute(tail, ROWS, [(i, i + 1) for i in range(ends)]),
            cells,
            lax.ppermute(head, ROWS, [(i + 1, i) for i in range(ends)]),
        ],
        axis=1,
    )


def shift_in(band, wide, moved, here):
    rows, cols, _ = band.shape
    edge = jnp.zeros((8, 128), f32)

    @pl.loop(0, rows)
    def _(i):
        wide[:8, :] = edge
        wide[8 + cols :, :] = edge
        wide[8 : 8 + cols, :] = band[i, :, here].astype(f32)
        for b in range(7):
            moved[b, i] = wide[b + 5 : b + 5 + cols, :]


def lanes_of(k):
    return pl.ds(pl.multiple_of(k * 128, 128), 128)


def tile_sums(moved, wide_taps, at, height):
    sums = [jnp.zeros((8, 128), f32) for _ in range(height)]
    for b in range(7):
        tap = [wide_taps[a * 7 + b] for a in range(7)]
        for i in range(height + 6):
            window = moved[b, i, at]
            for a in range(7):
                if 0 <= i - a < height:
                    sums[i - a] = sums[i - a] + window * tap[a]
    return sums


def widen_taps(taps, wide_taps, here):
    for i in range(49):
        wide_taps[i] = jnp.broadcast_to(taps[i : i + 1, here].astype(f32), (8, 128))


def conv_kernel(band, taps, out, wide, moved, wide_taps):
    height, cols, lanes = out.shape

    @pl.loop(0, lanes // 128)
    def _(k):
        here = lanes_of(k)
        shift_in(band, wide, moved, here)
        widen_taps(taps, wide_taps, here)

        @pl.loop(0, cols // 8)
        def _(t):
            at = pl.ds(pl.multiple_of(t * 8, 8), 8)
            for r, value in enumerate(tile_sums(moved, wide_taps, at, height)):
                out[r, at, here] = value


def back_kernel(band, taps, scaled, *refs):
    out, wide, moved, wide_taps, grad, grad_rows = refs[-6:]
    height, cols, lanes = out.shape
    upper = lax.broadcasted_iota(jnp.int32, (8, 128), 0) < REGION

    @pl.loop(0, lanes // 128)
    def _(k):
        here = lanes_of(k)
        shift_in(band, wide, moved, here)
        widen_taps(taps, wide_taps, here)
        for g in range(height // REGION):
            for t in range(cols // 8):
                at = g * (cols // REGION) + 2 * t
                grad[g, t * 8 : t * 8 + 8] = jnp.where(
                    upper, scaled[at : at + 1, here], scaled[at + 1 : at + 2, here]
                )

        @pl.loop(0, cols // 8)
        def _(t):
            at = pl.ds(pl.multiple_of(t * 8, 8), 8)
            for r, value in enumerate(tile_sums(moved, wide_taps, at, height)):
                grad_rows[r, at] = grad[r // REGION, at] + value

        out[:, :, here] = grad_rows[...].astype(bf16)


def terms_kernel(band, grad_b, loss, out, wide, moved, grad):
    height, cols, lanes = grad.shape
    out[48:, :] = jnp.broadcast_to(loss[:, :1], (out.shape[0] - 48, lanes))
    for r in range(height):
        grad[r] = grad_b[r].astype(f32)

    @pl.loop(0, lanes // 128)
    def _(k):
        here = lanes_of(k)
        shift_in(band, wide, moved, here)
        for b in range(7):

            def step(t, sums):
                sums = list(sums)
                at = pl.ds(pl.multiple_of(t * 8, 8), 8)
                g = [grad[r, at, here] for r in range(height)]
                for i in range(height + 6):
                    window = moved[b, i, at]
                    for a in range(7):
                        if 0 <= i - a < height:
                            sums[a] = sums[a] + window * g[i - a]
                return tuple(sums)

            sums = lax.fori_loop(0, cols // 8, step, (jnp.zeros((8, 128), f32),) * 7)
            for a in range(7):
                out[a * 7 + b : a * 7 + b + 1, here] = jnp.sum(sums[a], axis=0, keepdims=True)


def conv_scratch(rows, cols):
    return [pltpu.VMEM((cols + 16, 128), f32), pltpu.VMEM((7, rows, cols, 128), f32)]


def conv_forward(band, taps):
    rows, cols, channels = band.shape
    lanes = channels // 4
    return pl.pallas_call(
        conv_kernel,
        grid=(4,),
        in_specs=[
            pl.BlockSpec((rows, cols, lanes), lambda i: (0, 0, i)),
            pl.BlockSpec((49, lanes), lambda i: (0, i)),
        ],
        out_specs=pl.BlockSpec((rows - 6, cols, lanes), lambda i: (0, 0, i)),
        out_shape=jax.ShapeDtypeStruct((rows - 6, cols, channels), f32),
        scratch_shapes=conv_scratch(rows, cols) + [pltpu.VMEM((49, 8, 128), f32)],
        name="depthwise",
    )(band, taps)


def conv_backward(band, taps, scaled, k, parts, before):
    rows, cols, channels = band.shape
    lanes = channels // parts
    return pl.pallas_call(
        back_kernel,
        grid=(1,),
        in_specs=[
            pl.BlockSpec((rows, cols, lanes), lambda i: (0, 0, k)),
            pl.BlockSpec((49, lanes), lambda i: (0, k)),
            pl.BlockSpec((scaled.shape[0], lanes), lambda i: (0, k)),
        ]
        + [ANY] * len(before),
        out_specs=pl.BlockSpec((rows - 6, cols, lanes), lambda i: (0, 0, k)),
        out_shape=jax.ShapeDtypeStruct((rows - 6, cols, channels), bf16),
        input_output_aliases={3: 0} if before else {},
        scratch_shapes=conv_scratch(rows, cols)
        + [
            pltpu.VMEM((49, 8, 128), f32),
            pltpu.VMEM(((rows - 6) // REGION, cols, 128), f32),
            pltpu.VMEM((rows - 6, cols, 128), f32),
        ],
        name="depthwise_back",
    )(band, taps, scaled, *before)


def kernel_terms(band, grad_conv, loss):
    height, cols, channels = grad_conv.shape
    lanes = channels // 4
    return pl.pallas_call(
        terms_kernel,
        grid=(4,),
        in_specs=[
            pl.BlockSpec((height + 6, cols, lanes), lambda i: (0, 0, i)),
            pl.BlockSpec((height, cols, lanes), lambda i: (0, 0, i)),
            pl.BlockSpec((1, 128), lambda i: (0, 0)),
        ],
        out_specs=pl.BlockSpec((64, lanes), lambda i: (0, i)),
        out_shape=jax.ShapeDtypeStruct((64, channels), f32),
        scratch_shapes=conv_scratch(height + 6, cols) + [pltpu.VMEM((height, cols, lanes), f32)],
        name="kernel_terms",
    )(band, grad_conv, loss)


def gather_tokens(message):
    near = [message] + [fetch(message, "z_hi", 4, d) for d in (1, 2, 3)]
    near = jnp.concatenate(near, axis=1)
    ahead = fetch(near, "x", 4, 1)
    behind = fetch(near, "x", 4, 3)
    far = fetch(near, "x", 4, 2)
    return jnp.concatenate([near, ahead, far, behind], axis=1)


def spread_over(value, axes):
    count = lax.axis_size(axes)
    return lax.all_to_all(jnp.broadcast_to(value[None], (count,) + value.shape), axes, 0, 0)


def own_first(own, other):
    first = lax.axis_index("core") == 0
    return jnp.where(
        first, jnp.concatenate([own, other], axis=1), jnp.concatenate([other, own], axis=1)
    )


def total_over_all(values, work):
    width = values.shape[1] // 2
    first = lax.axis_index("core") == 0
    left, right = values[:, :width], values[:, width:]
    part = jnp.where(first, left, right) + fetch(jnp.where(first, right, left), "core", 2, 1)
    part = lax.all_to_all(part.reshape(16, -1, width), ("x", "y"), 0, 0)
    done = work(0)
    part, done = lax.optimization_barrier((part, done))
    part = spread_over(jnp.sum(part, axis=0), ("z_hi", "z_lo"))
    done = work(1, done)
    part, done = lax.optimization_barrier((part, done))
    part = spread_over(jnp.sum(part, axis=0), ("x", "y"))
    done = work(2, done)
    part, done = lax.optimization_barrier((part, done))
    part = part.reshape(-1, width)
    return own_first(part, fetch(part, "core", 2, 1)), done


def params(name, megabytes):
    return dict(
        name=name, compiler_params=pltpu.CompilerParams(vmem_limit_bytes=megabytes << 20)
    )


def body(features, kernel, ln_gain, layer_scale, w_in, w_out, pairs, negatives):
    height, breadth, channels = (features.shape[1], features.shape[2], features.shape[3])
    pixels = height * breadth
    reg_rows, reg_cols = (height // REGION, breadth // REGION)
    tokens = reg_rows * reg_cols
    hidden_width = w_in.shape[1]
    z, x, y, core = (lax.axis_index(name) for name in ("z_hi", "x", "y", "core"))
    idx = jnp.stack([z, x, y, lax.axis_index("z_lo"), core]).astype(jnp.int32)

    rimmed = padded_rows(features, 3)
    in_pieces, out_pieces, rimmed = gather_weights(w_in, w_out, rimmed)
    taps = kernel.reshape(49, channels)
    conv_rows = conv_forward(rimmed[0], taps).reshape(-1, channels)
    centred = conv_rows - jnp.mean(conv_rows, axis=-1, keepdims=True)
    spread = jnp.sqrt(jnp.mean(centred * centred, axis=-1, keepdims=True) + eps_layer)
    unit_rows = centred / spread
    normed = (unit_rows * ln_gain).astype(bf16)
    spread = jnp.broadcast_to(spread, (pixels, 128))
    in_pieces[3], normed, unit_rows, spread = lax.optimization_barrier(
        (in_pieces[3], normed, unit_rows, spread)
    )
    in_pieces, out_pieces = both_cores(in_pieces), both_cores(out_pieces)

    half = hidden_width // 2
    slope, pooled_hidden = pl.pallas_call(
        first_kernel,
        out_shape=(
            jax.ShapeDtypeStruct((2, pixels, half), f32),
            jax.ShapeDtypeStruct((2, 2 * tokens, half), bf16),
        ),
        in_specs=[SMEM, pl.BlockSpec()] + [ANY] * 8,
        scratch_shapes=[
            pltpu.VMEM((2, channels, half), bf16),
            pltpu.SemaphoreType.DMA((2,)),
        ],
        **params("expand_rows", 48),
    )(idx, normed, *in_pieces)

    width = channels // 2
    unit_tok, inv_norm, tokens_b = pl.pallas_call(
        second_kernel,
        out_shape=(
            jax.ShapeDtypeStruct((tokens, channels), f32),
            jax.ShapeDtypeStruct((tokens, 128), f32),
            jax.ShapeDtypeStruct((tokens, channels), bf16),
        ),
        in_specs=[SMEM] + [pl.BlockSpec()] * 3 + [ANY] * 8,
        scratch_shapes=[
            pltpu.VMEM((2, 4, 4, 4, hidden_width // 64, width), bf16),
            pltpu.VMEM((2, tokens, width), f32),
            pltpu.SemaphoreType.DMA((2,)),
        ],
        **params("pool_tokens", 32),
    )(
        idx,
        pooled_hidden,
        features.reshape(pixels, channels),
        layer_scale.reshape(1, channels),
        *out_pieces,
    )

    message = jnp.concatenate(
        [
            tokens_b.reshape(reg_rows, reg_cols, channels),
            jnp.pad(negatives[0].astype(bf16), ((0, 0), (0, 0), (0, 128 - NEG))),
        ],
        axis=2,
    )
    gathered = gather_tokens(message)
    slot = jnp.arange(16, dtype=jnp.int32)
    image = ((z + slot % 4) % 4) * 4 + (x + slot // 4) % 4
    columns = jnp.arange(reg_cols, dtype=jnp.int32)
    ids = (image[:, None] * reg_cols + columns[None, :]).reshape(1, -1).astype(f32)
    positive = (pairs[image][:, None] * reg_cols + columns[None, :]).reshape(-1, 1)
    positive = jnp.broadcast_to(positive, (positive.shape[0], 128)).astype(f32)

    grad_conv, scaled, loss_part = pl.pallas_call(
        third_kernel,
        out_shape=(
            jax.ShapeDtypeStruct((pixels, channels), bf16),
            jax.ShapeDtypeStruct((tokens, channels), f32),
            jax.ShapeDtypeStruct((1, 128), f32),
        ),
        in_specs=[SMEM] + [pl.BlockSpec()] * 8 + [ANY] * 18,
        scratch_shapes=[
            pltpu.VMEM((2, 4, 4, 4, hidden_width // 64, width), bf16),
            pltpu.VMEM((2, channels, half), bf16),
            pltpu.VMEM((2, pixels, half), f32),
            pltpu.VMEM((pixels, channels), f32),
            pltpu.VMEM((2, tokens, width), bf16),
            pltpu.VMEM((2, 3 * tokens, half), bf16),
            pltpu.VMEM((pixels, channels), f32),
            pltpu.SemaphoreType.DMA((2,)),
            pltpu.SemaphoreType.DMA((2,)),
            pltpu.SemaphoreType.DMA((2,)),
        ],
        **params("loss_and_back", 58),
    )(
        idx,
        gathered,
        positive,
        ids,
        unit_tok,
        inv_norm,
        layer_scale.reshape(1, channels),
        ln_gain.reshape(1, channels),
        spread,
        slope,
        unit_rows,
        *out_pieces,
        *in_pieces,
    )

    grad_conv = grad_conv.reshape(1, height, breadth, channels)
    local = kernel_terms(rimmed[0], grad_conv[0], loss_part)
    grad_rim, local = lax.optimization_barrier((padded_rows(grad_conv, 3), local))
    flipped = kernel[::-1, ::-1].reshape(49, channels)

    def back(k, *before):
        return conv_backward(grad_rim[0], flipped, scaled, k, 3, before)

    summed, grad_features = total_over_all(local, back)
    grad_features = grad_features[None]

    grad_kernel = summed[:49].reshape(7, 7, channels)
    token_count = lax.axis_size(AXES) * tokens
    loss = summed[49, 0] / float(token_count)
    return (grad_features, grad_kernel, loss)


def solution(mesh):
    split = Mesh(mesh.devices.reshape(4, 4, 4, 2, 2), AXES)
    return jax.shard_map(
        body,
        mesh=split,
        in_specs=(
            P(DP, ROWS, None, None),
            P(),
            P(),
            P(),
            P(AXES, None),
            P(AXES, None),
            P(),
            P(DP, ROWS, None, None),
        ),
        out_specs=(P(DP, ROWS, None, None), P(), P()),
        check_vma=False,
    )
```

```python
import jax
import jax.numpy as jnp
from jax import lax
from jax.experimental import pallas as pl
from jax.experimental.pallas import tpu as pltpu
from jax.sharding import Mesh, PartitionSpec as P

REGION = 4
NEG = 8
loss_scale = 1024.0
inv_temp = 16.0
eps_layer = 1e-06
eps_norm = 1e-06

AXES = ("z_hi", "x", "y", "z_lo", "core")
DP = ("z_hi", "x")
ROWS = ("y", "z_lo", "core")
bf16 = jnp.bfloat16
f32 = jnp.float32
ANY = pl.BlockSpec(memory_space=pl.ANY)
SMEM = pl.BlockSpec(memory_space=pltpu.SMEM)


def fetch(value, axis, count, distance):
    return lax.ppermute(value, axis, [((i + distance) % count, i) for i in range(count)])


def toward(value, axis, sign):
    pairs = []
    for i in range(4):
        for core in range(2):
            step = sign if core == 0 else -sign
            pairs.append((((i + step) % 4) * 2 + core, i * 2 + core))
    return lax.ppermute(value, (axis, "core"), pairs)


def ring(value, axis):
    near = toward(value, axis, 1)
    value, near = lax.optimization_barrier((value, near))
    return [value, near, toward(value, axis, -1), toward(near, axis, 1)]


def placed(pieces, position, dim):
    shape = [1] * (pieces[0].ndim + 1)
    shape[dim] = 4
    slot = jnp.arange(4).reshape(shape)
    whole = jnp.expand_dims(pieces[0], dim)
    for piece, distance in zip(pieces[1:], distances(lax.axis_index("core"))[1:]):
        whole = jnp.where(slot == (position + distance) % 4, jnp.expand_dims(piece, dim), whole)
    return whole


def distances(core):
    near = 1 + 2 * core
    return (0, near, 4 - near, 2)


def both_cores(pieces):
    return list(pieces) + [fetch(piece, "core", 2, 1) for piece in pieces]


def along_z(w_in, w_out):
    rows, width = w_in.shape[0], w_in.shape[1] // 2
    narrow = w_out.shape[1] // 2
    halves = [
        jnp.concatenate(
            [
                w_in[:, c * width : (c + 1) * width],
                w_out[:rows, c * narrow : (c + 1) * narrow],
                w_out[rows:, c * narrow : (c + 1) * narrow],
            ],
            axis=1,
        )
        for c in range(2)
    ]
    low_core, low_z = lax.axis_index("core") == 0, lax.axis_index("z_lo") == 0
    keep = jnp.where(low_core, halves[0], halves[1])
    got = fetch(jnp.where(low_core, halves[1], halves[0]), "core", 2, 1)
    pair = jnp.where(low_core, jnp.stack([keep, got]), jnp.stack([got, keep]))
    got = fetch(pair, "z_lo", 2, 1)
    quad = jnp.where(low_z, jnp.concatenate([pair, got]), jnp.concatenate([got, pair]))
    got = placed(ring(quad, "z_hi"), lax.axis_index("z_hi"), 0).reshape(16, rows, -1)
    near_in = got[:, :, :width].reshape(4, 4 * rows, width)
    near_out = jnp.concatenate(
        [got[:, :, width : width + narrow], got[:, :, width + narrow :]], axis=1
    ).reshape(4, 8 * rows, narrow)
    return near_in, near_out


def gather_weights(w_in, w_out, rimmed):
    near_in, near_out = along_z(w_in, w_out)
    middle_in = placed(ring(near_in, "y"), lax.axis_index("y"), 1)
    middle_in = middle_in.reshape(4, -1, near_in.shape[2])
    middle_out = placed(ring(near_out, "x"), lax.axis_index("x"), 1)
    pieces_in = ring(middle_in, "x")
    rimmed, _ = lax.optimization_barrier((rimmed, pieces_in[1]))
    pieces_out = ring(middle_out, "y")
    return pieces_in, pieces_out, rimmed


def copies_in(idx, pieces, held, sems):
    x = idx[1]
    for core in range(2):
        far = distances((idx[4] + core) % 2)
        for distance, piece in zip(far, pieces[core * 4 : core * 4 + 4]):
            rows = piece.shape[1]
            for i in range(piece.shape[0]):
                at = (i * 4 + (x + distance) % 4) * rows
                pltpu.make_async_copy(
                    piece.at[i],
                    held.at[core, pl.ds(pl.multiple_of(at, rows), rows), :],
                    sems.at[core],
                ).start()


def copies_out(idx, pieces, held, sems):
    y = idx[2]
    for core in range(2):
        far = distances((idx[4] + core) % 2)
        for distance, piece in zip(far, pieces[core * 4 : core * 4 + 4]):
            pltpu.make_async_copy(
                piece, held.at[core, :, :, (y + distance) % 4], sems.at[core]
            ).start()


def arrive(held, sems, core):
    pltpu.make_async_copy(held.at[core], held.at[core], sems.at[core]).wait()


def region_of(pixel):
    return ((pixel >> 7) << 3) + ((pixel & 31) >> 2)


def split2(value):
    high = value.astype(bf16)
    return high, (value - high.astype(f32)).astype(bf16)


def split3(value):
    high = value.astype(bf16)
    rest = value - high.astype(f32)
    mid = rest.astype(bf16)
    return high, mid, (rest - mid.astype(f32)).astype(bf16)


def pool_matrix(tokens, pixels):
    token = lax.broadcasted_iota(jnp.int32, (tokens, pixels), 0)
    pixel = lax.broadcasted_iota(jnp.int32, (tokens, pixels), 1)
    return jnp.where(region_of(pixel) == token, 1.0 / 16.0, 0.0).astype(bf16)


def dot(a, b):
    return jnp.dot(a, b, preferred_element_type=f32)


def dot_t(a, b):
    return lax.dot_general(a, b, (((1,), (1,)), ((), ())), preferred_element_type=f32)


def first_kernel(idx, normed, *refs):
    pieces, (slope, pooled, held, sems) = refs[:8], refs[8:]
    copies_in(idx, pieces, held, sems)
    pixels = normed.shape[0]
    tokens = pooled.shape[1] // 2
    steps = held.shape[2] // 512

    @pl.loop(0, 2)
    def _(core):
        arrive(held, sems, core)
        at = (idx[4] + core) % 2

        @pl.loop(0, steps)
        def _(step):
            lanes = pl.ds(pl.multiple_of(step * 512, 512), 512)
            pre = dot(normed[...], held[core, :, lanes])
            cdf = 0.5 * (1.0 + lax.erf(pre * 0.7071067811865476))
            density = jnp.exp(-0.5 * pre * pre) * 0.3989422804014327
            hidden = (pre * cdf).astype(bf16)
            slope[at, :, lanes] = cdf + pre * density
            high, low = split2(dot(pool_matrix(tokens, pixels), hidden))
            pooled[at, :tokens, lanes] = high
            pooled[at, tokens:, lanes] = low


def second_kernel(idx, hidden, feats, scale, *refs):
    pieces, (unit, norm, token, held, mixed, sems) = refs[:8], refs[8:]
    copies_out(idx, pieces, held, sems)
    tokens = unit.shape[0]
    base = dot(pool_matrix(tokens, feats.shape[0]), feats[...])
    half, width = hidden.shape[2], held.shape[5]
    @pl.loop(0, 2)
    def _(core):
        arrive(held, sems, core)
        at = (idx[4] + core) % 2
        low = held[core, :2].reshape(half, width)
        high = held[core, 2:].reshape(half, width)
        both = dot(hidden[0], low) + dot(hidden[1], high)
        mixed[at] = both[:tokens] + both[tokens:]

    full = jnp.concatenate([mixed[0], mixed[1]], axis=1)
    pool = base + scale[...] * full
    inv = lax.rsqrt(jnp.sum(pool * pool, axis=1, keepdims=True) + eps_norm)
    unit[...] = pool * inv
    norm[...] = jnp.broadcast_to(inv, norm.shape)
    token[...] = (pool * inv).astype(bf16)


def third_kernel(
    idx, keys, positive, ids, unit, norm, scale, gain, spread, slope_hbm, rows_hbm, *refs
):
    out_pieces, in_pieces = refs[:8], refs[8:16]
    (grad_conv, scaled, loss, held_out, held_in, slope, rows, mix, hid, total_ref) = refs[16:26]
    sem_out, sem_in, sem = refs[26:]
    copies_out(idx, out_pieces, held_out, sem_out)
    copies_in(idx, in_pieces, held_in, sem_in)
    copy_slope = pltpu.make_async_copy(slope_hbm, slope, sem.at[0])
    copy_slope.start()
    copy_rows = pltpu.make_async_copy(rows_hbm, rows, sem.at[1])
    copy_rows.start()
    token_grads, losses = [], []
    channels = unit.shape[1]
    for r in range(keys.shape[0]):
        key = keys[r, :, :channels]
        others = keys[r, :, channels:].astype(f32)
        count = key.shape[0]
        similar = dot_t(key, key)
        hits, logits = [], []
        for n in range(NEG + 1):
            hit = (positive[:, :1] if n == 0 else others[:, n - 1 : n]) == ids[...]
            hits.append(hit)
            logits.append(
                inv_temp * jnp.sum(jnp.where(hit, similar, 0.0), axis=1, keepdims=True)
            )
        exps = [jnp.exp(value) for value in logits]
        total = exps[0]
        for value in exps[1:]:
            total = total + value
        weight = jnp.zeros((count, count), f32)
        for n in range(NEG + 1):
            coef = loss_scale * inv_temp * (exps[n] / total - (1.0 if n == 0 else 0.0))
            weight = weight + jnp.where(hits[n], coef, 0.0)
        own = weight[:8] + jnp.transpose(weight)[:8]
        high, mid, low = split3(own)
        token_grads.append(dot(high, key) + dot(mid, key) + dot(low, key))
        losses.append((jnp.log(total) - logits[0])[:8])
    loss[...] = jnp.broadcast_to(
        jnp.sum(losses[0] + losses[1], axis=0, keepdims=True), loss.shape
    )
    grad_tok = jnp.concatenate(token_grads, axis=0)
    unit_v = unit[...]
    grad_pool = (grad_tok - unit_v * jnp.sum(unit_v * grad_tok, axis=1, keepdims=True)) * norm[
        :, :1
    ]
    spread_grad = grad_pool / 16.0
    scaled[...] = spread_grad
    grad_mix = (scale[...] * spread_grad).astype(bf16)
    width = held_out.shape[5]
    mix[0] = grad_mix[:, :width]
    mix[1] = grad_mix[:, width:]
    for core in range(2):
        arrive(held_out, sem_out, core)
    half = held_in.shape[2]
    tokens = grad_mix.shape[0]
    quarter = half // 2

    @pl.loop(0, 4)
    def _(z):
        part = jnp.zeros((quarter, tokens), f32)
        for core in range(2):
            at = (idx[4] + core) % 2
            part = part + dot_t(held_out[core, z].reshape(quarter, width), mix[at])
        lanes = pl.ds(pl.multiple_of((z & 1) * quarter, 128), quarter)
        for i, piece in enumerate(split3(jnp.transpose(part))):
            hid[z >> 1, i * tokens : (i + 1) * tokens, lanes] = piece

    copy_slope.wait()
    pixels = rows.shape[0]
    total_ref[...] = jnp.zeros(total_ref.shape, f32)
    @pl.loop(0, 2)
    def _(core):
        arrive(held_in, sem_in, core)
        at = (idx[4] + core) % 2

        @pl.loop(0, half // 512)
        def _(step):
            lanes = pl.ds(pl.multiple_of(step * 512, 512), 512)
            pixel = lax.broadcasted_iota(jnp.int32, (pixels, 3 * tokens), 0)
            token = lax.broadcasted_iota(jnp.int32, (pixels, 3 * tokens), 1) & (tokens - 1)
            expand = jnp.where(region_of(pixel) == token, 1.0, 0.0).astype(bf16)
            wide = dot(expand, hid[at, :, lanes])
            grad_pre = (wide * slope[at, :, lanes]).astype(bf16)
            total_ref[...] += dot_t(grad_pre, held_in[core, :, lanes])

    copy_rows.wait()
    grad_unit = total_ref[...] * gain[...]
    unit_rows = rows[...]
    mean_one = jnp.mean(grad_unit, axis=1, keepdims=True)
    mean_two = jnp.mean(grad_unit * unit_rows, axis=1, keepdims=True)
    grad_conv[...] = ((grad_unit - mean_one - unit_rows * mean_two) / spread[:, :1]).astype(bf16)


def padded_rows(cells, width):
    count = lax.axis_size(ROWS)
    ends = count - 1
    head = cells[:, :width]
    tail = cells[:, cells.shape[1] - width :]
    return jnp.concatenate(
        [
            lax.ppermute(tail, ROWS, [(i, i + 1) for i in range(ends)]),
            cells,
            lax.ppermute(head, ROWS, [(i + 1, i) for i in range(ends)]),
        ],
        axis=1,
    )


def shift_in(band, wide, moved, here):
    rows, cols, _ = band.shape
    edge = jnp.zeros((8, 128), f32)

    @pl.loop(0, rows)
    def _(i):
        wide[:8, :] = edge
        wide[8 + cols :, :] = edge
        wide[8 : 8 + cols, :] = band[i, :, here].astype(f32)
        for b in range(7):
            moved[b, i] = wide[b + 5 : b + 5 + cols, :]


def lanes_of(k):
    return pl.ds(pl.multiple_of(k * 128, 128), 128)


def tile_sums(moved, wide_taps, at, height):
    sums = [jnp.zeros((8, 128), f32) for _ in range(height)]
    for b in range(7):
        tap = [wide_taps[a * 7 + b] for a in range(7)]
        for i in range(height + 6):
            window = moved[b, i, at]
            for a in range(7):
                if 0 <= i - a < height:
                    sums[i - a] = sums[i - a] + window * tap[a]
    return sums


def widen_taps(taps, wide_taps, here):
    for i in range(49):
        wide_taps[i] = jnp.broadcast_to(taps[i : i + 1, here].astype(f32), (8, 128))


def conv_kernel(band, taps, out, wide, moved, wide_taps):
    height, cols, lanes = out.shape

    @pl.loop(0, lanes // 128)
    def _(k):
        here = lanes_of(k)
        shift_in(band, wide, moved, here)
        widen_taps(taps, wide_taps, here)

        @pl.loop(0, cols // 8)
        def _(t):
            at = pl.ds(pl.multiple_of(t * 8, 8), 8)
            for r, value in enumerate(tile_sums(moved, wide_taps, at, height)):
                out[r, at, here] = value


def back_kernel(band, taps, scaled, *refs):
    out, wide, moved, wide_taps, grad, grad_rows = refs[-6:]
    height, cols, lanes = out.shape
    upper = lax.broadcasted_iota(jnp.int32, (8, 128), 0) < REGION

    @pl.loop(0, lanes // 128)
    def _(k):
        here = lanes_of(k)
        shift_in(band, wide, moved, here)
        widen_taps(taps, wide_taps, here)
        for g in range(height // REGION):
            for t in range(cols // 8):
                at = g * (cols // REGION) + 2 * t
                grad[g, t * 8 : t * 8 + 8] = jnp.where(
                    upper, scaled[at : at + 1, here], scaled[at + 1 : at + 2, here]
                )

        @pl.loop(0, cols // 8)
        def _(t):
            at = pl.ds(pl.multiple_of(t * 8, 8), 8)
            for r, value in enumerate(tile_sums(moved, wide_taps, at, height)):
                grad_rows[r, at] = grad[r // REGION, at] + value

        out[:, :, here] = grad_rows[...].astype(bf16)


def terms_kernel(band, grad_b, loss, out, wide, moved, grad):
    height, cols, lanes = grad.shape
    out[48:, :] = jnp.broadcast_to(loss[:, :1], (out.shape[0] - 48, lanes))
    for r in range(height):
        grad[r] = grad_b[r].astype(f32)

    @pl.loop(0, lanes // 128)
    def _(k):
        here = lanes_of(k)
        shift_in(band, wide, moved, here)
        for b in range(7):

            def step(t, sums):
                sums = list(sums)
                at = pl.ds(pl.multiple_of(t * 8, 8), 8)
                g = [grad[r, at, here] for r in range(height)]
                for i in range(height + 6):
                    window = moved[b, i, at]
                    for a in range(7):
                        if 0 <= i - a < height:
                            sums[a] = sums[a] + window * g[i - a]
                return tuple(sums)

            sums = lax.fori_loop(0, cols // 8, step, (jnp.zeros((8, 128), f32),) * 7)
            for a in range(7):
                out[a * 7 + b : a * 7 + b + 1, here] = jnp.sum(sums[a], axis=0, keepdims=True)


def conv_scratch(rows, cols):
    return [pltpu.VMEM((cols + 16, 128), f32), pltpu.VMEM((7, rows, cols, 128), f32)]


def conv_forward(band, taps):
    rows, cols, channels = band.shape
    lanes = channels // 4
    return pl.pallas_call(
        conv_kernel,
        grid=(4,),
        in_specs=[
            pl.BlockSpec((rows, cols, lanes), lambda i: (0, 0, i)),
            pl.BlockSpec((49, lanes), lambda i: (0, i)),
        ],
        out_specs=pl.BlockSpec((rows - 6, cols, lanes), lambda i: (0, 0, i)),
        out_shape=jax.ShapeDtypeStruct((rows - 6, cols, channels), f32),
        scratch_shapes=conv_scratch(rows, cols) + [pltpu.VMEM((49, 8, 128), f32)],
        name="depthwise",
    )(band, taps)


def conv_backward(band, taps, scaled, k, parts, before):
    rows, cols, channels = band.shape
    lanes = channels // parts
    return pl.pallas_call(
        back_kernel,
        grid=(1,),
        in_specs=[
            pl.BlockSpec((rows, cols, lanes), lambda i: (0, 0, k)),
            pl.BlockSpec((49, lanes), lambda i: (0, k)),
            pl.BlockSpec((scaled.shape[0], lanes), lambda i: (0, k)),
        ]
        + [ANY] * len(before),
        out_specs=pl.BlockSpec((rows - 6, cols, lanes), lambda i: (0, 0, k)),
        out_shape=jax.ShapeDtypeStruct((rows - 6, cols, channels), bf16),
        input_output_aliases={3: 0} if before else {},
        scratch_shapes=conv_scratch(rows, cols)
        + [
            pltpu.VMEM((49, 8, 128), f32),
            pltpu.VMEM(((rows - 6) // REGION, cols, 128), f32),
            pltpu.VMEM((rows - 6, cols, 128), f32),
        ],
        name="depthwise_back",
    )(band, taps, scaled, *before)


def kernel_terms(band, grad_conv, loss):
    height, cols, channels = grad_conv.shape
    lanes = channels // 4
    return pl.pallas_call(
        terms_kernel,
        grid=(4,),
        in_specs=[
            pl.BlockSpec((height + 6, cols, lanes), lambda i: (0, 0, i)),
            pl.BlockSpec((height, cols, lanes), lambda i: (0, 0, i)),
            pl.BlockSpec((1, 128), lambda i: (0, 0)),
        ],
        out_specs=pl.BlockSpec((64, lanes), lambda i: (0, i)),
        out_shape=jax.ShapeDtypeStruct((64, channels), f32),
        scratch_shapes=conv_scratch(height + 6, cols) + [pltpu.VMEM((height, cols, lanes), f32)],
        name="kernel_terms",
    )(band, grad_conv, loss)


def gather_tokens(message):
    near = [message] + [fetch(message, "z_hi", 4, d) for d in (1, 2, 3)]
    near = jnp.concatenate(near, axis=1)
    ahead = fetch(near, "x", 4, 1)
    behind = fetch(near, "x", 4, 3)
    far = fetch(near, "x", 4, 2)
    return jnp.concatenate([near, ahead, far, behind], axis=1)


def spread_over(value, axes):
    count = lax.axis_size(axes)
    return lax.all_to_all(jnp.broadcast_to(value[None], (count,) + value.shape), axes, 0, 0)


def own_first(own, other):
    first = lax.axis_index("core") == 0
    return jnp.where(
        first, jnp.concatenate([own, other], axis=1), jnp.concatenate([other, own], axis=1)
    )


def total_over_all(values, work):
    width = values.shape[1] // 2
    first = lax.axis_index("core") == 0
    left, right = values[:, :width], values[:, width:]
    part = jnp.where(first, left, right) + fetch(jnp.where(first, right, left), "core", 2, 1)
    chips = ("z_hi", "x", "y", "z_lo")
    part = lax.all_to_all(part.reshape(128, 1, -1), chips, 0, 0)
    done = work(0)
    part, done = lax.optimization_barrier((part, done))
    part = spread_over(jnp.sum(part, axis=0), chips)
    done = work(1, done)
    part, done = lax.optimization_barrier((part, done))
    part = part.reshape(-1, width)
    return own_first(part, fetch(part, "core", 2, 1)), done


def params(name, megabytes):
    return dict(
        name=name, compiler_params=pltpu.CompilerParams(vmem_limit_bytes=megabytes << 20)
    )


def body(features, kernel, ln_gain, layer_scale, w_in, w_out, pairs, negatives):
    height, breadth, channels = (features.shape[1], features.shape[2], features.shape[3])
    pixels = height * breadth
    reg_rows, reg_cols = (height // REGION, breadth // REGION)
    tokens = reg_rows * reg_cols
    hidden_width = w_in.shape[1]
    z, x, y, core = (lax.axis_index(name) for name in ("z_hi", "x", "y", "core"))
    idx = jnp.stack([z, x, y, lax.axis_index("z_lo"), core]).astype(jnp.int32)

    rimmed = padded_rows(features, 3)
    in_pieces, out_pieces, rimmed = gather_weights(w_in, w_out, rimmed)
    taps = kernel.reshape(49, channels)
    conv_rows = conv_forward(rimmed[0], taps).reshape(-1, channels)
    centred = conv_rows - jnp.mean(conv_rows, axis=-1, keepdims=True)
    spread = jnp.sqrt(jnp.mean(centred * centred, axis=-1, keepdims=True) + eps_layer)
    unit_rows = centred / spread
    normed = (unit_rows * ln_gain).astype(bf16)
    spread = jnp.broadcast_to(spread, (pixels, 128))
    in_pieces[3], normed, unit_rows, spread = lax.optimization_barrier(
        (in_pieces[3], normed, unit_rows, spread)
    )
    in_pieces, out_pieces = both_cores(in_pieces), both_cores(out_pieces)

    half = hidden_width // 2
    slope, pooled_hidden = pl.pallas_call(
        first_kernel,
        out_shape=(
            jax.ShapeDtypeStruct((2, pixels, half), f32),
            jax.ShapeDtypeStruct((2, 2 * tokens, half), bf16),
        ),
        in_specs=[SMEM, pl.BlockSpec()] + [ANY] * 8,
        scratch_shapes=[
            pltpu.VMEM((2, channels, half), bf16),
            pltpu.SemaphoreType.DMA((2,)),
        ],
        **params("expand_rows", 48),
    )(idx, normed, *in_pieces)

    width = channels // 2
    unit_tok, inv_norm, tokens_b = pl.pallas_call(
        second_kernel,
        out_shape=(
            jax.ShapeDtypeStruct((tokens, channels), f32),
            jax.ShapeDtypeStruct((tokens, 128), f32),
            jax.ShapeDtypeStruct((tokens, channels), bf16),
        ),
        in_specs=[SMEM] + [pl.BlockSpec()] * 3 + [ANY] * 8,
        scratch_shapes=[
            pltpu.VMEM((2, 4, 4, 4, hidden_width // 64, width), bf16),
            pltpu.VMEM((2, tokens, width), f32),
            pltpu.SemaphoreType.DMA((2,)),
        ],
        **params("pool_tokens", 32),
    )(
        idx,
        pooled_hidden,
        features.reshape(pixels, channels),
        layer_scale.reshape(1, channels),
        *out_pieces,
    )

    message = jnp.concatenate(
        [
            tokens_b.reshape(reg_rows, reg_cols, channels),
            jnp.pad(negatives[0].astype(bf16), ((0, 0), (0, 0), (0, 128 - NEG))),
        ],
        axis=2,
    )
    gathered = gather_tokens(message)
    slot = jnp.arange(16, dtype=jnp.int32)
    image = ((z + slot % 4) % 4) * 4 + (x + slot // 4) % 4
    columns = jnp.arange(reg_cols, dtype=jnp.int32)
    ids = (image[:, None] * reg_cols + columns[None, :]).reshape(1, -1).astype(f32)
    positive = (pairs[image][:, None] * reg_cols + columns[None, :]).reshape(-1, 1)
    positive = jnp.broadcast_to(positive, (positive.shape[0], 128)).astype(f32)

    grad_conv, scaled, loss_part = pl.pallas_call(
        third_kernel,
        out_shape=(
            jax.ShapeDtypeStruct((pixels, channels), bf16),
            jax.ShapeDtypeStruct((tokens, channels), f32),
            jax.ShapeDtypeStruct((1, 128), f32),
        ),
        in_specs=[SMEM] + [pl.BlockSpec()] * 8 + [ANY] * 18,
        scratch_shapes=[
            pltpu.VMEM((2, 4, 4, 4, hidden_width // 64, width), bf16),
            pltpu.VMEM((2, channels, half), bf16),
            pltpu.VMEM((2, pixels, half), f32),
            pltpu.VMEM((pixels, channels), f32),
            pltpu.VMEM((2, tokens, width), bf16),
            pltpu.VMEM((2, 3 * tokens, half), bf16),
            pltpu.VMEM((pixels, channels), f32),
            pltpu.SemaphoreType.DMA((2,)),
            pltpu.SemaphoreType.DMA((2,)),
            pltpu.SemaphoreType.DMA((2,)),
        ],
        **params("loss_and_back", 58),
    )(
        idx,
        gathered,
        positive,
        ids,
        unit_tok,
        inv_norm,
        layer_scale.reshape(1, channels),
        ln_gain.reshape(1, channels),
        spread,
        slope,
        unit_rows,
        *out_pieces,
        *in_pieces,
    )

    grad_conv = grad_conv.reshape(1, height, breadth, channels)
    local = kernel_terms(rimmed[0], grad_conv[0], loss_part)
    grad_rim, local = lax.optimization_barrier((padded_rows(grad_conv, 3), local))
    flipped = kernel[::-1, ::-1].reshape(49, channels)

    def back(k, *before):
        return conv_backward(grad_rim[0], flipped, scaled, k, 2, before)

    summed, grad_features = total_over_all(local, back)
    grad_features = grad_features[None]

    grad_kernel = summed[:49].reshape(7, 7, channels)
    token_count = lax.axis_size(AXES) * tokens
    loss = summed[49, 0] / float(token_count)
    return (grad_features, grad_kernel, loss)


def solution(mesh):
    split = Mesh(mesh.devices.reshape(4, 4, 4, 2, 2), AXES)
    return jax.shard_map(
        body,
        mesh=split,
        in_specs=(
            P(DP, ROWS, None, None),
            P(),
            P(),
            P(),
            P(AXES, None),
            P(AXES, None),
            P(),
            P(DP, ROWS, None, None),
        ),
        out_specs=(P(DP, ROWS, None, None), P(), P()),
        check_vma=False,
    )
```
